32 devices in a mesh: slices: 2 (over y), gx: 4 (over z), gy: 2 (over x), gz: 2 (over core).
Axes of the slice: x: 2, y: 2, z: 4, core: 2. Of those that a mesh axis runs over, the one named last changes fastest.
Arguments:
- gauge_links: float32 [3, 2, 3, 3, 24, 48, 128], P(None, None, None, None, ('slices', 'gx'), ('gy', 'gz')), parts along dimension 4, may hold values from -1.8 to 2.8
Outputs:
- rotated_links: float32 [3, 2, 3, 3, 24, 48, 128], P(None, None, None, None, ('slices', 'gx'), ('gy', 'gz')), parts along dimension 4
The draws below stay inside these ranges and needn't reach their ends.
There are 2 independent parts, one for each index of `slices`. The reference program is written for one: setup_inputs(seed, part) draws one part's arguments, and reference() takes and returns one part's arrays. A program takes and returns all parts, laid end to end along the dimension named above; each array names one. Nothing has to cross between parts.
All inputs are finite; a program needn't handle non-finite values.
Results may differ from the reference program's by a relative error of at most 0.000084.
Values sent between devices are 32-bit elements; how exact they have to be, the bound alone decides.
A program may use at most 128 MiB of HBM per device.

```python
import math
import jax
import jax.numpy as jnp
from jax import lax

CX = 3
NZ = 128
NX = 12
NY = 48
N_GX = 4


def draw_gauge_links(key, part):
    full_shape = (3, 2, 3, 3, NX, NY, NZ)
    identity = jnp.eye(3, dtype=jnp.float32)[None, None, :, :, None, None, None]
    real_select = jnp.array([1.0, 0.0], jnp.float32)[None, :, None, None, None, None, None]
    fluctuation = jnp.clip(0.3 * jax.random.normal(key, full_shape, jnp.float32), -1.8, 1.8)
    return identity * real_select + fluctuation


def setup_inputs(seed: int = 0, part: int = 0) -> dict:
    key_list = jax.random.split(jax.random.key(seed), 2)
    part_keys = jax.random.split(jax.random.fold_in(key_list[1], part), 2)
    return {
        "gauge_links": draw_gauge_links(jax.random.fold_in(jax.random.fold_in(key_list[1], part), 71), part),
    }


SMEAR_RHO = 0.1
HALF_STEP = -0.04


def complex_product(left_mat, right_mat):
    total_real = 0.0
    total_imag = 0.0
    for middle in range(3):
        left_real = left_mat[0][:, middle][:, None]
        left_imag = left_mat[1][:, middle][:, None]
        right_real = right_mat[0][middle][None]
        right_imag = right_mat[1][middle][None]
        total_real = total_real + left_real * right_real - left_imag * right_imag
        total_imag = total_imag + left_real * right_imag + left_imag * right_real
    return jnp.stack([total_real, total_imag])


def dagger(matrix_in):
    return jnp.stack([jnp.swapaxes(matrix_in[0], 0, 1), -jnp.swapaxes(matrix_in[1], 0, 1)])


def identity_like(sample):
    eye_mat = jnp.eye(3, dtype=sample.dtype).reshape((3, 3) + (1,) * (sample.ndim - 3))
    real_part = eye_mat * jnp.ones(sample.shape[3:], sample.dtype)
    return jnp.stack([real_part, jnp.zeros_like(real_part)])


def antihermitian(matrix_in):
    halved = 0.5 * (matrix_in - dagger(matrix_in))
    trace_third = (halved[1, 0, 0] + halved[1, 1, 1] + halved[1, 2, 2]) / 3.0
    return halved - identity_like(halved)[::-1] * trace_third


def components(matrix_in):
    return jnp.stack([matrix_in[1, 0, 0], matrix_in[1, 1, 1], matrix_in[0, 0, 1], matrix_in[1, 0, 1],
                      matrix_in[0, 0, 2], matrix_in[1, 0, 2], matrix_in[0, 1, 2], matrix_in[1, 1, 2]])


def from_components(values):
    zero_field = jnp.zeros_like(values[0])
    real_rows = [[zero_field, values[2], values[4]], [-values[2], zero_field, values[6]], [-values[4], -values[6], zero_field]]
    imag_rows = [[values[0], values[3], values[5]], [values[3], values[1], values[7]], [values[5], values[7], -values[0] - values[1]]]
    return jnp.stack([jnp.stack([jnp.stack(matrix_row) for matrix_row in real_rows]),
                      jnp.stack([jnp.stack(matrix_row) for matrix_row in imag_rows])])


def matrix_exp(generator):
    scaled = generator * 0.5
    identity = identity_like(generator)
    series = identity + scaled / 6.0
    for divisor in (5.0, 4.0, 3.0, 2.0, 1.0):
        series = identity + complex_product(scaled, series) / divisor
    return complex_product(series, series)


def stout_smear(padded):
    inner_sizes = [padded.shape[4] - 2, padded.shape[5] - 2, padded.shape[6] - 2]
    unit_steps = ((1, 0, 0), (0, 1, 0), (0, 0, 1))

    def link_at(direction, shift_by):
        return padded[direction][:, :, :,
                                 1 + shift_by[0]:1 + shift_by[0] + inner_sizes[0],
                                 1 + shift_by[1]:1 + shift_by[1] + inner_sizes[1],
                                 1 + shift_by[2]:1 + shift_by[2] + inner_sizes[2]]

    anchor = (0, 0, 0)
    smeared_links = []
    for along_dir in range(3):
        current = link_at(along_dir, anchor)
        staple_sum = jnp.zeros_like(current)
        for cross_dir in range(3):
            if cross_dir == along_dir:
                continue
            upward = unit_steps[cross_dir]
            forward = unit_steps[along_dir]
            downward = tuple(-component for component in upward)
            diagonal = tuple(forward[coord_pos] - upward[coord_pos] for coord_pos in range(3))
            upper_staple = complex_product(complex_product(link_at(cross_dir, anchor), link_at(along_dir, upward)),
                                           dagger(link_at(cross_dir, forward)))
            lower_staple = complex_product(complex_product(dagger(link_at(cross_dir, downward)), link_at(along_dir, downward)),
                                           link_at(cross_dir, diagonal))
            staple_sum = staple_sum + upper_staple + lower_staple
        generator = SMEAR_RHO * antihermitian(complex_product(staple_sum, dagger(current)))
        smeared_links.append(complex_product(matrix_exp(generator), current))
    return jnp.stack(smeared_links)


def laplace_factor(freq_x, freq_y, freq_z, count_x, count_y, count_z):
    sine_x = jnp.sin(math.pi * freq_x / count_x)
    sine_y = jnp.sin(math.pi * freq_y / count_y)
    sine_z = jnp.sin(math.pi * freq_z / count_z)
    squared = (4.0 * (sine_x * sine_x)[:, None, None] + 4.0 * (sine_y * sine_y)[None, :, None]
               + 4.0 * (sine_z * sine_z)[None, None, :])
    positive = squared > 0.0
    return jnp.where(positive, 12.0 / jnp.where(positive, squared, 1.0), 0.0)


def rotate_links(transform_here, neighbours, smeared_block):
    rotated = [complex_product(complex_product(transform_here, smeared_block[direction]), dagger(neighbours[direction]))
               for direction in range(3)]
    return jnp.stack(rotated)


def reference(gauge_links):
    padded = jnp.pad(gauge_links, ((0, 0),) * 4 + ((1, 1),) * 3, mode="wrap")
    slab_ids = jnp.arange(N_GX, dtype=jnp.int32)

    def smear_slab(slab_index):
        offset = slab_index * CX
        slab_links = lax.dynamic_slice_in_dim(padded, offset, CX + 2, 4)
        return stout_smear(slab_links)

    smeared = lax.map(smear_slab, slab_ids)
    smeared = jnp.moveaxis(smeared, 0, 4).reshape((3, 2, 3, 3, NX, NY, NZ))
    parts_a = [components(antihermitian(smeared[direction])) for direction in range(3)]
    divergence = (parts_a[0] - jnp.roll(parts_a[0], 1, axis=1)
                  + parts_a[1] - jnp.roll(parts_a[1], 1, axis=2)
                  + parts_a[2] - jnp.roll(parts_a[2], 1, axis=3))
    spectrum = jnp.fft.fftn(divergence, axes=(1, 2, 3))
    factor = laplace_factor(jnp.arange(NX, dtype=jnp.float32), jnp.arange(NY, dtype=jnp.float32),
                            jnp.arange(NZ, dtype=jnp.float32), NX, NY, NZ)
    accel_field = jnp.fft.ifftn(spectrum * factor, axes=(1, 2, 3)).real
    accel_ext = jnp.concatenate([accel_field, accel_field[:, :1]], axis=1)

    def rotate_slab(slab_index):
        offset = slab_index * CX
        accel_piece = lax.dynamic_slice_in_dim(accel_ext, offset, CX + 1, 1)
        links_piece = lax.dynamic_slice_in_dim(smeared, offset, CX, 4)
        transform_g = matrix_exp(from_components(accel_piece) * HALF_STEP)
        transform_here = transform_g[:, :, :, :-1]
        neighbours = [transform_g[:, :, :, 1:], jnp.roll(transform_here, -1, axis=4), jnp.roll(transform_here, -1, axis=5)]
        return rotate_links(transform_here, neighbours, links_piece)

    rotated = lax.map(rotate_slab, slab_ids)
    return jnp.moveaxis(rotated, 0, 4).reshape((3, 2, 3, 3, NX, NY, NZ))
```

```python
import functools
import math

import jax
import jax.numpy as jnp
import numpy as np
from jax import lax
from jax.experimental import pallas as pl
from jax.experimental.pallas import tpu as pltpu
from jax.sharding import PartitionSpec as P

SMEAR_RHO = 0.1
HALF_STEP = -0.04
MESH = pl.DeviceIdType.MESH
HIGHEST = lax.Precision.HIGHEST
VMEM = pl.BlockSpec(memory_space=pltpu.VMEM)
ANY = pl.BlockSpec(memory_space=pl.ANY)


def laplace_factor(freq_x, freq_y, freq_z, count_x, count_y, count_z):
    sine_x = jnp.sin(math.pi * freq_x / count_x)
    sine_y = jnp.sin(math.pi * freq_y / count_y)
    sine_z = jnp.sin(math.pi * freq_z / count_z)
    squared = (
        4.0 * (sine_x * sine_x)[:, None, None]
        + 4.0 * (sine_y * sine_y)[None, :, None]
        + 4.0 * (sine_z * sine_z)[None, None, :]
    )
    positive = squared > 0.0
    return jnp.where(positive, 12.0 / jnp.where(positive, squared, 1.0), 0.0)


def dft_tables(length):
    positions = jnp.arange(length, dtype=jnp.int32)
    phases = positions[:, None] * positions[None, :] % length
    angles = phases.astype(jnp.float32) * (2.0 * math.pi / length)
    return (jnp.cos(angles), jnp.sin(angles))


def transform(spectrum, axis_pos, direction_sign):
    length = spectrum.shape[axis_pos]
    cosine_table, sine_table = dft_tables(length)
    highest = lax.Precision.HIGHEST
    real_part = jnp.moveaxis(spectrum[0], axis_pos - 1, -1)
    imag_part = jnp.moveaxis(spectrum[1], axis_pos - 1, -1)
    out_real = jnp.dot(real_part, cosine_table, precision=highest) + direction_sign * jnp.dot(
        imag_part, sine_table, precision=highest
    )
    out_imag = jnp.dot(imag_part, cosine_table, precision=highest) - direction_sign * jnp.dot(
        real_part, sine_table, precision=highest
    )
    return jnp.moveaxis(jnp.stack([out_real, out_imag]), -1, axis_pos)


def general_solve(payload, rows_x, rows_y, depth_z):
    spectrum = jnp.stack([payload, jnp.zeros_like(payload)])
    fields_n = spectrum.shape[1]
    spectrum = transform(spectrum, 4, 1.0)
    spectrum = lax.all_to_all(spectrum, ("gy", "gz"), split_axis=4, concat_axis=3, tiled=True)
    groups_y = lax.axis_size(("gy", "gz"))
    span_z = spectrum.shape[4]
    blocks = spectrum.reshape((2, fields_n, rows_x + 1, groups_y, rows_y + 1, span_z))
    carried = jnp.roll(blocks[:, :, :, :, rows_y], 1, axis=3)
    first_row = blocks[:, :, :, :, 0] - carried
    blocks = jnp.concatenate([first_row[:, :, :, :, None], blocks[:, :, :, :, 1:rows_y]], axis=4)
    spectrum = blocks.reshape((2, fields_n, rows_x + 1, groups_y * rows_y, span_z))
    spectrum = transform(spectrum, 3, 1.0)
    spectrum = lax.all_to_all(spectrum, "gx", split_axis=3, concat_axis=2, tiled=True)
    groups_x = lax.axis_size("gx")
    span_y = spectrum.shape[3]
    blocks = spectrum.reshape((2, fields_n, groups_x, rows_x + 1, span_y, span_z))
    carried = jnp.roll(blocks[:, :, :, rows_x], 1, axis=2)
    first_row = blocks[:, :, :, 0] - carried
    blocks = jnp.concatenate([first_row[:, :, :, None], blocks[:, :, :, 1:rows_x]], axis=3)
    spectrum = blocks.reshape((2, fields_n, groups_x * rows_x, span_y, span_z))
    spectrum = transform(spectrum, 2, 1.0)
    length_x = groups_x * rows_x
    length_y = groups_y * rows_y
    freq_x = jnp.arange(length_x, dtype=jnp.float32)
    freq_y = (lax.axis_index("gx") * span_y + jnp.arange(span_y, dtype=jnp.int32)).astype(
        jnp.float32
    )
    freq_z = (lax.axis_index(("gy", "gz")) * span_z + jnp.arange(span_z, dtype=jnp.int32)).astype(
        jnp.float32
    )
    factor = laplace_factor(freq_x, freq_y, freq_z, length_x, length_y, depth_z) / float(
        length_x * length_y * depth_z
    )
    spectrum = spectrum * factor
    spectrum = transform(spectrum, 2, -1.0)
    blocks = spectrum.reshape((2, fields_n, groups_x, rows_x, span_y, span_z))
    following = jnp.roll(blocks[:, :, :, :1], -1, axis=2)
    spectrum = jnp.concatenate([blocks, following], axis=3).reshape(
        (2, fields_n, groups_x * (rows_x + 1), span_y, span_z)
    )
    spectrum = lax.all_to_all(spectrum, "gx", split_axis=2, concat_axis=3, tiled=True)
    spectrum = transform(spectrum, 3, -1.0)
    blocks = spectrum.reshape((2, fields_n, rows_x + 1, groups_y, rows_y, span_z))
    following = jnp.roll(blocks[:, :, :, :, :1], -1, axis=3)
    spectrum = jnp.concatenate([blocks, following], axis=4).reshape(
        (2, fields_n, rows_x + 1, groups_y * (rows_y + 1), span_z)
    )
    spectrum = lax.all_to_all(spectrum, ("gy", "gz"), split_axis=3, concat_axis=4, tiled=True)
    spectrum = transform(spectrum, 4, -1.0)
    return spectrum[0]


def cmul(a, b):
    return a[0] * b[0] - a[1] * b[1], a[0] * b[1] + a[1] * b[0]


def cadd(a, b):
    return a[0] + b[0], a[1] + b[1]


def conj(a):
    return a[0], -a[1]


def dot3(pairs):
    real = imag = None
    for a, b, flip_a, flip_b in pairs:
        rr, ii = a[0] * b[0], a[1] * b[1]
        ri, ir = a[0] * b[1], a[1] * b[0]
        r = rr - ii if flip_a == flip_b else rr + ii
        i = {(0, 0): lambda: ri + ir, (0, 1): lambda: ir - ri, (1, 0): lambda: ri - ir}[(flip_a, flip_b)]()
        real = r if real is None else real + r
        imag = i if imag is None else imag + i
    return real, imag


def mat_mul(a, b):
    return [[dot3([(a[r][m], b[m][c], 0, 0) for m in range(3)]) for c in range(3)] for r in range(3)]


def mat_mul_dag(a, b):
    return [[dot3([(a[r][m], b[c][m], 0, 1) for m in range(3)]) for c in range(3)] for r in range(3)]


def dag_mat_mul(a, b):
    return [[dot3([(a[m][r], b[m][c], 1, 0) for m in range(3)]) for c in range(3)] for r in range(3)]


def anti_parts(m):
    third = (m[0][0][1] + m[1][1][1] + m[2][2][1]) * (1.0 / 3.0)
    out = [m[0][0][1] - third, m[1][1][1] - third]
    for r, c in ((0, 1), (0, 2), (1, 2)):
        out.append(0.5 * (m[r][c][0] - m[c][r][0]))
        out.append(0.5 * (m[r][c][1] + m[c][r][1]))
    return out


def exp_parts(parts, scale):
    v = [0.5 * scale * p for p in parts]
    h0, h1 = v[0], v[1]
    h2 = -h0 - h1
    h01, h02, h12 = (v[3], -v[2]), (v[5], -v[4]), (v[7], -v[6])
    n01, n02, n12 = [h[0] * h[0] + h[1] * h[1] for h in (h01, h02, h12)]
    s0, s1, s2 = h0 * h0, h1 * h1, h2 * h2
    k00, k11, k22 = s0 + n01 + n02, s1 + n01 + n12, s2 + n02 + n12
    p02 = cmul(h01, h12)
    q = cmul(h02, conj(h12))
    w = cmul(conj(h01), h02)
    k01 = (q[0] - h2 * h01[0], q[1] - h2 * h01[1])
    k02 = (p02[0] - h1 * h02[0], p02[1] - h1 * h02[1])
    k12 = (w[0] - h0 * h12[0], w[1] - h0 * h12[1])
    t = 0.5 * (k00 + k11 + k22)
    d = h0 * h1 * h2 + 2.0 * (p02[0] * h02[0] + p02[1] * h02[1]) - h0 * n12 - h1 * n02 - h2 * n01
    t2 = t * t
    q0 = (1.0 - d * d * (1.0 / 720.0), d * (t * (1.0 / 120.0) - 1.0 / 6.0))
    q1 = (d * (1.0 / 24.0 - t * (1.0 / 360.0)), 1.0 - t * (1.0 / 6.0) + t2 * (1.0 / 120.0))
    q2 = (t * (1.0 / 24.0) - 0.5 - t2 * (1.0 / 720.0), d * (1.0 / 120.0))
    q00, q01, q02, q11, q12, q22 = cmul(q0, q0), cmul(q0, q1), cmul(q0, q2), cmul(q1, q1), cmul(q1, q2), cmul(q2, q2)
    e0 = [q00[n] + 2.0 * d * q12[n] for n in range(2)]
    e1 = [2.0 * (q01[n] + t * q12[n]) + d * q22[n] for n in range(2)]
    e2 = [2.0 * q02[n] + q11[n] + t * q22[n] for n in range(2)]
    out = [[None] * 3 for _ in range(3)]
    for r, (h, k) in enumerate(((h0, k00), (h1, k11), (h2, k22))):
        out[r][r] = (e0[0] + e1[0] * h + e2[0] * k, e0[1] + e1[1] * h + e2[1] * k)
    for r, c, h, k in ((0, 1, h01, k01), (0, 2, h02, k02), (1, 2, h12, k12)):
        out[r][c] = cadd(cmul(e1, h), cmul(e2, k))
        out[c][r] = cadd(cmul(e1, conj(h)), cmul(e2, conj(k)))
    return out


def mat_map(fn, m):
    return [[(fn(e[0]), fn(e[1])) for e in row] for row in m]


def load_mat(ref, base, x, row):
    return [
        [tuple(ref[base + 9 * part + 3 * r + c, x, row : row + 8, :] for part in range(2)) for c in range(3)]
        for r in range(3)
    ]


def forward_z(value):
    return pltpu.roll(value, value.shape[1] - 1, 1)


def backward_z(value):
    return pltpu.roll(value, 1, 1)


def staple_kernel(l_ref, hx_ref, hy_ref, gu_ref, lx_ref, ly_ref, rim_ref, ext):
    rows_x, rows_y = l_ref.shape[1], l_ref.shape[2]

    def fill(n, _):
        ext[n, 0:rows_x, 0:rows_y, :] = l_ref[n]
        return 0

    lax.fori_loop(0, 54, fill, 0)

    def fill_x(n, _):
        ext[18 + n, rows_x, 0:rows_y, :] = hx_ref[n]
        return 0

    lax.fori_loop(0, 36, fill_x, 0)
    for n in range(36):
        target = n if n < 18 else n + 18
        for x in range(rows_x):
            ext[target, x, rows_y : rows_y + 1, :] = hy_ref[x, n : n + 1, :]

    def step(x, _):
        for row in (0, rows_y - 8):
            here = slice(row, row + 8)
            acc = [None] * 3

            def add(direction, parts, sign=1.0):
                if acc[direction] is None:
                    acc[direction] = parts if sign > 0 else [-p for p in parts]
                elif sign > 0:
                    acc[direction] = [p + q for p, q in zip(acc[direction], parts)]
                else:
                    acc[direction] = [p - q for p, q in zip(acc[direction], parts)]

            for i, j in ((0, 1), (0, 2), (1, 2)):
                ui, uj = load_mat(ext, 18 * i, x, row), load_mat(ext, 18 * j, x, row)
                if j == 1:
                    ui_j = load_mat(ext, 18 * i, x, row + 1)
                else:
                    ui_j = mat_map(forward_z, ui)
                if i == 0:
                    uj_i = load_mat(ext, 18 * j, x + 1, row)
                else:
                    uj_i = load_mat(ext, 18 * j, x, row + 1)
                b = mat_mul(ui, uj_i)
                a = mat_mul(uj, ui_j)
                plaquette = anti_parts(mat_mul_dag(a, b))
                add(i, plaquette)
                add(j, plaquette, -1.0)
                low_i = anti_parts(mat_mul_dag(dag_mat_mul(uj, b), ui_j))
                low_j = anti_parts(mat_mul_dag(dag_mat_mul(ui, a), uj_i))
                if j == 2:
                    add(i, [backward_z(p) for p in low_i])
                for parts, shift, slot in ((low_i, j, 0), (low_j, i, 0 if j == 1 else 8)):
                    for n, p in enumerate(parts):
                        if shift == 0:
                            lx_ref[slot + n, x, here, :] = p
                        elif shift == 1:
                            ly_ref[slot + n, x, row + 1 : row + 9, :] = p
                            if row:
                                rim_ref[x, slot + n : slot + n + 1, :] = p[7:8, :]
            for direction in range(3):
                for n in range(8):
                    gu_ref[8 * direction + n, x, here, :] = acc[direction][n]
        return 0

    lax.fori_loop(0, rows_x, step, 0)


def smear_kernel(fast, l_ref, gu_ref, lx_ref, ly_ref, rx_ref, ry_ref, table_ref, v_ref, s_ref, a0, a1, dz, pack):
    rows_x, rows_y = l_ref.shape[1], l_ref.shape[2]

    def step(x, _):
        before = jnp.maximum(x - 1, 0)
        for row in (0, rows_y - 8):
            here = slice(row, row + 8)
            top = lax.broadcasted_iota(jnp.int32, (8, 128), 0) == 0

            def low_x(n):
                return jnp.where(x == 0, rx_ref[n, here, :], lx_ref[n, before, here, :])

            def low_y(n):
                value = ly_ref[n, x, here, :]
                if row == 0:
                    value = jnp.where(top, ry_ref[x, n : n + 1, :], value)
                return value

            for direction in range(3):
                parts = []
                for n in range(8):
                    p = gu_ref[8 * direction + n, x, here, :]
                    if direction == 0:
                        p = p + low_y(n)
                    elif direction == 1:
                        p = p + low_x(n)
                    else:
                        p = p + low_x(8 + n) + low_y(8 + n)
                    parts.append(p)
                smeared = mat_mul(exp_parts(parts, SMEAR_RHO), load_mat(l_ref, 18 * direction, x, row))
                for r in range(3):
                    for c in range(3):
                        for part in range(2):
                            v_ref[18 * direction + 9 * part + 3 * r + c, x, here, :] = smeared[r][c][part]
                for n, p in enumerate(anti_parts(smeared)):
                    if direction == 0:
                        a0[n, x, here, :] = p
                    elif direction == 1:
                        a1[n, x, row + 1 : row + 9, :] = p
                    else:
                        dz[n, x, here, :] = p - backward_z(p)
        return 0

    lax.fori_loop(0, rows_x, step, 0)

    def divergence(n, _):
        pack[n] = jnp.zeros(pack.shape[1:], jnp.float32)
        for x in range(rows_x):
            total = a0[n, x] + dz[n, x] + a1[n, x, 1 : rows_y + 1, :]
            if x:
                total = total - a0[n, x - 1]
            lanes = slice(128 * (x // 2), 128 * (x // 2) + 128)
            pack[n, x % 2, 0:rows_y, lanes] = total
            pack[n, x % 2, 1:rows_y, lanes] = pack[n, x % 2, 1:rows_y, lanes] - a1[n, x, 1:rows_y, :]
            pack[n, x % 2, rows_y : rows_y + 1, lanes] = a1[n, x, rows_y : rows_y + 1, :]
        pack[n, 1, 0:rows_y, 128:256] = a0[n, rows_x - 1]
        return 0

    lax.fori_loop(0, 8, divergence, 0)
    if fast:
        out = jnp.dot(
            pack[...].reshape(256, 256), table_ref[...], precision=HIGHEST, preferred_element_type=jnp.float32
        )
        for half in range(2):
            s_ref[:, half] = out[:, 128 * half : 128 * half + 128].reshape(8, 2, 16, 128)
    else:
        s_ref[...] = pack[...]


def solve_kernel(r_ref, ty_ref, tyi_ref, cf_ref, ci_ref, f_ref, o_ref):
    half = lax.axis_index("gz")
    planes = []
    for gx in range(4):
        for xp in range(2):
            block = r_ref[4 * gx : 4 * gx + 4, xp].reshape(64, 128)
            planes.append(
                jnp.dot(ty_ref[...], block, precision=HIGHEST, preferred_element_type=jnp.float32)
            )
    turned = [pltpu.roll(p, 64, 1) for p in planes]
    modes = []
    for m in range(6):
        total = None
        for n in range(8):
            term = planes[n] * cf_ref[m, n, 0:1, :] + turned[n] * cf_ref[m, n, 1:2, :]
            total = term if total is None else total + term
        modes.append(total * f_ref[half, m])
    turned = [pltpu.roll(p, 64, 1) for p in modes]
    for gx in range(4):
        for xp in range(2):
            total = None
            for m in range(6):
                term = modes[m] * ci_ref[2 * gx + xp, m, 0:1, :] + turned[m] * ci_ref[2 * gx + xp, m, 1:2, :]
                total = term if total is None else total + term
            out = jnp.dot(tyi_ref[...], total, precision=HIGHEST, preferred_element_type=jnp.float32)
            o_ref[4 * gx : 4 * gx + 4, xp] = out.reshape(4, 16, 128)


def rotate_kernel(fast, q_ref, v_ref, table_ref, o_ref, acc, g):
    rows_x, rows_y = v_ref.shape[1], v_ref.shape[2]
    if fast:
        left = jnp.concatenate([q_ref[:, 0].reshape(256, 128), q_ref[:, 1].reshape(256, 128)], axis=1)
        out = jnp.dot(left, table_ref[...], precision=HIGHEST, preferred_element_type=jnp.float32)
        for part in range(2):
            acc[:, 2 * part : 2 * part + 2] = out[:, 128 * part : 128 * part + 128].reshape(8, 2, 16, 128)
        src = acc
    else:
        src = q_ref

    def exponent(x, _):
        for row in (0, 8):
            here = slice(row, row + 8)
            m = exp_parts([src[n, x, here, :] for n in range(8)], HALF_STEP)
            for r in range(3):
                for c in range(3):
                    for part in range(2):
                        g[9 * part + 3 * r + c, x, here, :] = m[r][c][part]
        return 0

    lax.fori_loop(0, rows_x + 1, exponent, 0)

    def step(x, _):
        for row in (0, rows_y - 8):
            here = slice(row, row + 8)
            centre = load_mat(g, 0, x, row)
            for direction in range(3):
                if direction == 0:
                    other = load_mat(g, 0, x + 1, row)
                elif direction == 1:
                    other = load_mat(g, 0, x, row + 1)
                else:
                    other = mat_map(forward_z, centre)
                out = mat_mul_dag(mat_mul(centre, load_mat(v_ref, 18 * direction, x, row)), other)
                for r in range(3):
                    for c in range(3):
                        for part in range(2):
                            o_ref[18 * direction + 9 * part + 3 * r + c, x, here, :] = out[r][c][part]
        return 0

    lax.fori_loop(0, rows_x, step, 0)


def neighbour(axis_sizes, step_x, step_y):
    n_x, n_y, n_z = axis_sizes
    gx = lax.axis_index("gx")
    block = lax.axis_index("gy") * n_z + lax.axis_index("gz")
    if step_x:
        return {"gx": lax.rem(gx + n_x + step_x, n_x)}
    block = lax.rem(block + n_y * n_z + step_y, n_y * n_z)
    return {"gy": lax.div(block, n_z), "gz": lax.rem(block, n_z)}


def exchange_kernel(sizes, way, pick, sx_ref, sy_ref, rx_ref, ry_ref, send, recv):
    barrier = pltpu.get_barrier_semaphore()
    for device in (neighbour(sizes, -way, 0), neighbour(sizes, 0, -way)):
        pl.semaphore_signal(barrier, inc=1, device_id=device, device_id_type=MESH)
    pl.semaphore_wait(barrier, 2)
    first, count, x = pick
    copies = []
    for n, (src, dst, device) in enumerate(
        (
            (sx_ref.at[pl.ds(first, count), x], rx_ref, neighbour(sizes, way, 0)),
            (sy_ref, ry_ref, neighbour(sizes, 0, way)),
        )
    ):
        copies.append(
            pltpu.make_async_remote_copy(
                src_ref=src,
                dst_ref=dst,
                send_sem=send.at[n],
                recv_sem=recv.at[n],
                device_id=device,
                device_id_type=MESH,
            )
        )
        copies[-1].start()
    for copy in copies:
        copy.wait()


def exchange(sizes, way, pick, key, sx, sy):
    shapes = (
        jax.ShapeDtypeStruct((pick[1],) + sx.shape[2:], jnp.float32),
        jax.ShapeDtypeStruct(sy.shape, jnp.float32),
    )
    return pl.pallas_call(
        functools.partial(exchange_kernel, sizes, way, pick),
        out_shape=shapes,
        in_specs=[ANY, ANY],
        out_specs=(ANY, ANY),
        scratch_shapes=[pltpu.SemaphoreType.DMA((2,)), pltpu.SemaphoreType.DMA((2,))],
        compiler_params=pltpu.CompilerParams(collective_id=key, has_side_effects=True),
    )(sx, sy)


def swap_kernel(sizes, s_ref, r_ref, send, recv, local):
    n_x, n_y, n_z = sizes
    total = n_x * n_y * n_z
    me = (lax.axis_index("gx") * n_y + lax.axis_index("gy")) * n_z + lax.axis_index("gz")

    def device(index):
        return {
            "gx": lax.div(index, n_y * n_z),
            "gy": lax.rem(lax.div(index, n_z), n_y),
            "gz": lax.rem(index, n_z),
        }

    barrier = pltpu.get_barrier_semaphore()
    for offset in range(1, total):
        pl.semaphore_signal(
            barrier, inc=1, device_id=device(lax.rem(me + offset, total)), device_id_type=MESH
        )
    own = pltpu.make_async_copy(s_ref.at[me], r_ref.at[me], local)
    own.start()
    pl.semaphore_wait(barrier, total - 1)
    copies = []
    for offset in sorted(range(1, total), key=lambda o: -min(o, total - o)):
        peer = lax.rem(me + offset, total)
        copies.append(
            pltpu.make_async_remote_copy(
                src_ref=s_ref.at[peer],
                dst_ref=r_ref.at[me],
                send_sem=send.at[offset],
                recv_sem=recv.at[offset],
                device_id=device(peer),
                device_id_type=MESH,
            )
        )
        copies[-1].start()
    own.wait()
    for copy in copies:
        copy.wait()


def swap(sizes, key, blocks):
    total = blocks.shape[0]
    return pl.pallas_call(
        functools.partial(swap_kernel, sizes),
        out_shape=jax.ShapeDtypeStruct(blocks.shape, jnp.float32),
        in_specs=[ANY],
        out_specs=ANY,
        scratch_shapes=[
            pltpu.SemaphoreType.DMA((total,)),
            pltpu.SemaphoreType.DMA((total,)),
            pltpu.SemaphoreType.DMA,
        ],
        compiler_params=pltpu.CompilerParams(collective_id=key, has_side_effects=True),
    )(blocks)


def real_basis(length):
    x = np.arange(length)
    freq = np.zeros(length, np.int64)
    rows = np.zeros((length, length))
    rows[0] = 1.0 / math.sqrt(length)
    for n in range(1, length):
        k = (n + 1) // 2
        freq[n] = k
        angle = 2.0 * math.pi * ((k * x) % length) / length
        if 2 * k == length:
            rows[n] = np.cos(angle) / math.sqrt(length)
        else:
            rows[n] = (np.cos(angle) if n % 2 else np.sin(angle)) * math.sqrt(2.0 / length)
    return rows, 4.0 * np.sin(math.pi * freq / length) ** 2


def tables():
    tz, pz = real_basis(128)
    ty, py = real_basis(48)
    tx, px = real_basis(12)
    wide = np.zeros((2, 128, 2, 2, 64))
    for p in range(2):
        wide[p, :, :, p, :] = tz.T.reshape(128, 2, 64)
    wide = wide.reshape(256, 256)
    fy = np.zeros((48, 4, 16))
    iy = np.zeros((4, 16, 48))
    for b in range(4):
        fy[:, b, :12] = ty[:, 12 * b : 12 * b + 12]
        fy[:, b, 12] = -ty[:, (12 * b + 12) % 48]
        for r in range(13):
            iy[b, r] = ty[:, (12 * b + r) % 48]
    cf = np.zeros((6, 8, 2, 2, 64))
    ci = np.zeros((8, 6, 2, 2, 64))
    factor = np.zeros((2, 6, 48, 2, 64))
    for m in range(6):
        for q in range(2):
            squared = px[m + 6 * q] + py[None, :, None] + pz.reshape(2, 1, 64)
            factor[:, m, :, q] = np.where(squared > 1e-9, 12.0 / np.where(squared > 1e-9, squared, 1.0), 0.0)
            for gx in range(4):
                for xp in range(2):
                    for turn in range(2):
                        x = xp + 2 * (q if turn == 0 else 1 - q)
                        kx = m + 6 * q
                        site = (3 * gx + x) % 12
                        cf[m, 2 * gx + xp, turn, q] = -tx[kx, site] if x == 3 else tx[kx, site]
                        back = m + 6 * (q if turn == 0 else 1 - q)
                        ci[2 * gx + xp, m, turn, q] = tx[back, (3 * gx + xp + 2 * q) % 12]
    flat = lambda t, shape: jnp.asarray(t.reshape(shape), jnp.float32)
    return (
        flat(wide, (256, 256)),
        flat(wide.T.copy(), (256, 256)),
        flat(fy, (48, 64)),
        flat(iy, (64, 48)),
        flat(cf, (6, 8, 2, 128)),
        flat(ci, (8, 6, 2, 128)),
        flat(factor, (2, 6, 48, 128)),
    )


def local(kernel, shapes, scratch, *operands):
    single = isinstance(shapes[0], int)
    out = pl.pallas_call(
        kernel,
        out_shape=tuple(jax.ShapeDtypeStruct(s, jnp.float32) for s in ((shapes,) if single else shapes)),
        in_specs=[VMEM] * len(operands),
        out_specs=tuple(VMEM for _ in ((shapes,) if single else shapes)),
        scratch_shapes=[pltpu.VMEM(s, jnp.float32) for s in scratch],
        compiler_params=pltpu.CompilerParams(vmem_limit_bytes=40 << 20),
    )(*operands)
    return out[0] if single else out


def shards(sizes, gauge_links):
    rows_x, rows_y, depth = gauge_links.shape[4:]
    fast = sizes == (4, 2, 2)
    wide, wide_back, fy, iy, cf, ci, factor = tables()
    links = gauge_links.reshape(54, rows_x, rows_y, depth)
    first = links[:, :, 0, :]
    edge = jnp.moveaxis(jnp.concatenate([first[:18], first[36:]], axis=0), 0, 1)
    hx, hy = exchange(sizes, -1, (18, 36, 0), 1, links, edge)
    gu, lx, ly, rim = local(
        staple_kernel,
        (
            (24, rows_x, rows_y, depth),
            (16, rows_x, rows_y, depth),
            (16, rows_x, rows_y + 1, depth),
            (rows_x, 16, depth),
        ),
        [(54, rows_x + 1, 16, depth)],
        links,
        hx,
        hy,
    )
    rx, ry = exchange(sizes, 1, (0, 16, rows_x - 1), 2, lx, rim)
    spectral = (8, 2, 2, 16, 128) if fast else (8, 2, 16, 256)
    smeared, blocks = local(
        functools.partial(smear_kernel, fast),
        ((54, rows_x, rows_y, depth), spectral),
        [
            (8, rows_x, rows_y, depth),
            (8, rows_x, rows_y + 1, depth),
            (8, rows_x, rows_y, depth),
            (8, 2, 16, 256),
        ],
        links,
        gu,
        lx,
        ly,
        rx,
        ry,
        wide,
    )
    if fast:
        received = swap(sizes, 3, blocks.reshape(16, 2, 16, 128))
        solved = local(solve_kernel, (16, 2, 16, 128), [], received, fy, iy, cf, ci, factor)
        accel = swap(sizes, 4, solved).reshape(8, 2, 2, 16, 128)
    else:
        used = blocks[:, :, : rows_y + 1]
        payload = jnp.concatenate([used[..., :depth], used[..., depth:]], axis=1)
        accel = general_solve(payload, rows_x, rows_y, depth)
        accel = jnp.pad(accel, ((0, 0), (0, 0), (0, 16 - accel.shape[2]), (0, 0)))
    rotated = local(
        functools.partial(rotate_kernel, fast),
        (54, rows_x, rows_y, depth),
        [(8, 4, 16, 128), (18, rows_x + 1, 16, depth)],
        accel,
        smeared,
        wide_back,
    )
    return rotated.reshape(gauge_links.shape)


def solution(mesh):
    sizes = (mesh.shape["gx"], mesh.shape["gy"], mesh.shape["gz"])
    return jax.shard_map(
        functools.partial(shards, sizes),
        mesh=mesh,
        in_specs=(P(None, None, None, None, ("slices", "gx"), ("gy", "gz"), None),),
        out_specs=P(None, None, None, None, ("slices", "gx"), ("gy", "gz"), None),
        check_vma=False,
    )
```

```python
import functools
import math

import jax
import jax.numpy as jnp
import numpy as np
from jax import lax
from jax.experimental import pallas as pl
from jax.experimental.pallas import tpu as pltpu
from jax.sharding import PartitionSpec as P

SMEAR_RHO = 0.1
HALF_STEP = -0.04
MESH = pl.DeviceIdType.MESH
HIGHEST = lax.Precision.HIGHEST
VMEM = pl.BlockSpec(memory_space=pltpu.VMEM)
ANY = pl.BlockSpec(memory_space=pl.ANY)


def laplace_factor(freq_x, freq_y, freq_z, count_x, count_y, count_z):
    sine_x = jnp.sin(math.pi * freq_x / count_x)
    sine_y = jnp.sin(math.pi * freq_y / count_y)
    sine_z = jnp.sin(math.pi * freq_z / count_z)
    squared = (
        4.0 * (sine_x * sine_x)[:, None, None]
        + 4.0 * (sine_y * sine_y)[None, :, None]
        + 4.0 * (sine_z * sine_z)[None, None, :]
    )
    positive = squared > 0.0
    return jnp.where(positive, 12.0 / jnp.where(positive, squared, 1.0), 0.0)


def dft_tables(length):
    positions = jnp.arange(length, dtype=jnp.int32)
    phases = positions[:, None] * positions[None, :] % length
    angles = phases.astype(jnp.float32) * (2.0 * math.pi / length)
    return (jnp.cos(angles), jnp.sin(angles))


def transform(spectrum, axis_pos, direction_sign):
    length = spectrum.shape[axis_pos]
    cosine_table, sine_table = dft_tables(length)
    highest = lax.Precision.HIGHEST
    real_part = jnp.moveaxis(spectrum[0], axis_pos - 1, -1)
    imag_part = jnp.moveaxis(spectrum[1], axis_pos - 1, -1)
    out_real = jnp.dot(real_part, cosine_table, precision=highest) + direction_sign * jnp.dot(
        imag_part, sine_table, precision=highest
    )
    out_imag = jnp.dot(imag_part, cosine_table, precision=highest) - direction_sign * jnp.dot(
        real_part, sine_table, precision=highest
    )
    return jnp.moveaxis(jnp.stack([out_real, out_imag]), -1, axis_pos)


def general_solve(payload, rows_x, rows_y, depth_z):
    spectrum = jnp.stack([payload, jnp.zeros_like(payload)])
    fields_n = spectrum.shape[1]
    spectrum = transform(spectrum, 4, 1.0)
    spectrum = lax.all_to_all(spectrum, ("gy", "gz"), split_axis=4, concat_axis=3, tiled=True)
    groups_y = lax.axis_size(("gy", "gz"))
    span_z = spectrum.shape[4]
    blocks = spectrum.reshape((2, fields_n, rows_x + 1, groups_y, rows_y + 1, span_z))
    carried = jnp.roll(blocks[:, :, :, :, rows_y], 1, axis=3)
    first_row = blocks[:, :, :, :, 0] - carried
    blocks = jnp.concatenate([first_row[:, :, :, :, None], blocks[:, :, :, :, 1:rows_y]], axis=4)
    spectrum = blocks.reshape((2, fields_n, rows_x + 1, groups_y * rows_y, span_z))
    spectrum = transform(spectrum, 3, 1.0)
    spectrum = lax.all_to_all(spectrum, "gx", split_axis=3, concat_axis=2, tiled=True)
    groups_x = lax.axis_size("gx")
    span_y = spectrum.shape[3]
    blocks = spectrum.reshape((2, fields_n, groups_x, rows_x + 1, span_y, span_z))
    carried = jnp.roll(blocks[:, :, :, rows_x], 1, axis=2)
    first_row = blocks[:, :, :, 0] - carried
    blocks = jnp.concatenate([first_row[:, :, :, None], blocks[:, :, :, 1:rows_x]], axis=3)
    spectrum = blocks.reshape((2, fields_n, groups_x * rows_x, span_y, span_z))
    spectrum = transform(spectrum, 2, 1.0)
    length_x = groups_x * rows_x
    length_y = groups_y * rows_y
    freq_x = jnp.arange(length_x, dtype=jnp.float32)
    freq_y = (lax.axis_index("gx") * span_y + jnp.arange(span_y, dtype=jnp.int32)).astype(
        jnp.float32
    )
    freq_z = (lax.axis_index(("gy", "gz")) * span_z + jnp.arange(span_z, dtype=jnp.int32)).astype(
        jnp.float32
    )
    factor = laplace_factor(freq_x, freq_y, freq_z, length_x, length_y, depth_z) / float(
        length_x * length_y * depth_z
    )
    spectrum = spectrum * factor
    spectrum = transform(spectrum, 2, -1.0)
    blocks = spectrum.reshape((2, fields_n, groups_x, rows_x, span_y, span_z))
    following = jnp.roll(blocks[:, :, :, :1], -1, axis=2)
    spectrum = jnp.concatenate([blocks, following], axis=3).reshape(
        (2, fields_n, groups_x * (rows_x + 1), span_y, span_z)
    )
    spectrum = lax.all_to_all(spectrum, "gx", split_axis=2, concat_axis=3, tiled=True)
    spectrum = transform(spectrum, 3, -1.0)
    blocks = spectrum.reshape((2, fields_n, rows_x + 1, groups_y, rows_y, span_z))
    following = jnp.roll(blocks[:, :, :, :, :1], -1, axis=3)
    spectrum = jnp.concatenate([blocks, following], axis=4).reshape(
        (2, fields_n, rows_x + 1, groups_y * (rows_y + 1), span_z)
    )
    spectrum = lax.all_to_all(spectrum, ("gy", "gz"), split_axis=3, concat_axis=4, tiled=True)
    spectrum = transform(spectrum, 4, -1.0)
    return spectrum[0]


def cmul(a, b):
    return a[0] * b[0] - a[1] * b[1], a[0] * b[1] + a[1] * b[0]


def cadd(a, b):
    return a[0] + b[0], a[1] + b[1]


def conj(a):
    return a[0], -a[1]


def dot3(pairs):
    real = imag = None
    for a, b, flip_a, flip_b in pairs:
        rr, ii = a[0] * b[0], a[1] * b[1]
        ri, ir = a[0] * b[1], a[1] * b[0]
        r = rr - ii if flip_a == flip_b else rr + ii
        i = {(0, 0): lambda: ri + ir, (0, 1): lambda: ir - ri, (1, 0): lambda: ri - ir}[(flip_a, flip_b)]()
        real = r if real is None else real + r
        imag = i if imag is None else imag + i
    return real, imag


def mat_mul(a, b):
    return [[dot3([(a[r][m], b[m][c], 0, 0) for m in range(3)]) for c in range(3)] for r in range(3)]


def mat_mul_dag(a, b):
    return [[dot3([(a[r][m], b[c][m], 0, 1) for m in range(3)]) for c in range(3)] for r in range(3)]


def dag_mat_mul(a, b):
    return [[dot3([(a[m][r], b[m][c], 1, 0) for m in range(3)]) for c in range(3)] for r in range(3)]


def anti_parts(m):
    third = (m[0][0][1] + m[1][1][1] + m[2][2][1]) * (1.0 / 3.0)
    out = [m[0][0][1] - third, m[1][1][1] - third]
    for r, c in ((0, 1), (0, 2), (1, 2)):
        out.append(0.5 * (m[r][c][0] - m[c][r][0]))
        out.append(0.5 * (m[r][c][1] + m[c][r][1]))
    return out


def exp_parts(parts, scale):
    v = [0.5 * scale * p for p in parts]
    h0, h1 = v[0], v[1]
    h2 = -h0 - h1
    h01, h02, h12 = (v[3], -v[2]), (v[5], -v[4]), (v[7], -v[6])
    n01, n02, n12 = [h[0] * h[0] + h[1] * h[1] for h in (h01, h02, h12)]
    s0, s1, s2 = h0 * h0, h1 * h1, h2 * h2
    k00, k11, k22 = s0 + n01 + n02, s1 + n01 + n12, s2 + n02 + n12
    p02 = cmul(h01, h12)
    q = cmul(h02, conj(h12))
    w = cmul(conj(h01), h02)
    k01 = (q[0] - h2 * h01[0], q[1] - h2 * h01[1])
    k02 = (p02[0] - h1 * h02[0], p02[1] - h1 * h02[1])
    k12 = (w[0] - h0 * h12[0], w[1] - h0 * h12[1])
    t = 0.5 * (k00 + k11 + k22)
    d = h0 * h1 * h2 + 2.0 * (p02[0] * h02[0] + p02[1] * h02[1]) - h0 * n12 - h1 * n02 - h2 * n01
    t2 = t * t
    q0 = (1.0 - d * d * (1.0 / 720.0), d * (t * (1.0 / 120.0) - 1.0 / 6.0))
    q1 = (d * (1.0 / 24.0 - t * (1.0 / 360.0)), 1.0 - t * (1.0 / 6.0) + t2 * (1.0 / 120.0))
    q2 = (t * (1.0 / 24.0) - 0.5 - t2 * (1.0 / 720.0), d * (1.0 / 120.0))
    q00, q01, q02, q11, q12, q22 = cmul(q0, q0), cmul(q0, q1), cmul(q0, q2), cmul(q1, q1), cmul(q1, q2), cmul(q2, q2)
    e0 = [q00[n] + 2.0 * d * q12[n] for n in range(2)]
    e1 = [2.0 * (q01[n] + t * q12[n]) + d * q22[n] for n in range(2)]
    e2 = [2.0 * q02[n] + q11[n] + t * q22[n] for n in range(2)]
    out = [[None] * 3 for _ in range(3)]
    for r, (h, k) in enumerate(((h0, k00), (h1, k11), (h2, k22))):
        out[r][r] = (e0[0] + e1[0] * h + e2[0] * k, e0[1] + e1[1] * h + e2[1] * k)
    for r, c, h, k in ((0, 1, h01, k01), (0, 2, h02, k02), (1, 2, h12, k12)):
        out[r][c] = cadd(cmul(e1, h), cmul(e2, k))
        out[c][r] = cadd(cmul(e1, conj(h)), cmul(e2, conj(k)))
    return out


def mat_map(fn, m):
    return [[(fn(e[0]), fn(e[1])) for e in row] for row in m]


def load_mat(ref, base, x, row):
    return [
        [tuple(ref[base + 9 * part + 3 * r + c, x, row : row + 8, :] for part in range(2)) for c in range(3)]
        for r in range(3)
    ]


def forward_z(value):
    return pltpu.roll(value, value.shape[1] - 1, 1)


def backward_z(value):
    return pltpu.roll(value, 1, 1)


def staple_kernel(l_ref, hx_ref, hy_ref, gu_ref, lx_ref, ly_ref, rim_ref, ext):
    rows_x, rows_y = l_ref.shape[1], l_ref.shape[2]

    def fill(n, _):
        ext[n, 0:rows_x, 0:rows_y, :] = l_ref[n]
        return 0

    lax.fori_loop(0, 54, fill, 0)

    def fill_x(n, _):
        ext[18 + n, rows_x, 0:rows_y, :] = hx_ref[n]
        return 0

    lax.fori_loop(0, 36, fill_x, 0)
    for n in range(36):
        target = n if n < 18 else n + 18
        for x in range(rows_x):
            ext[target, x, rows_y : rows_y + 1, :] = hy_ref[x, n : n + 1, :]
    staple_planes(ext, gu_ref, lx_ref, ly_ref, rim_ref, lambda x: None)


def staple_planes(ext, gu_ref, lx_ref, ly_ref, rim_ref, arrive):
    rows_x, rows_y = gu_ref.shape[1], gu_ref.shape[2]

    def step(x, _):
        arrive(x)
        for row in (0, rows_y - 8):
            here = slice(row, row + 8)
            acc = [None] * 3

            def add(direction, parts, sign=1.0):
                if acc[direction] is None:
                    acc[direction] = parts if sign > 0 else [-p for p in parts]
                elif sign > 0:
                    acc[direction] = [p + q for p, q in zip(acc[direction], parts)]
                else:
                    acc[direction] = [p - q for p, q in zip(acc[direction], parts)]

            for i, j in ((0, 1), (0, 2), (1, 2)):
                ui, uj = load_mat(ext, 18 * i, x, row), load_mat(ext, 18 * j, x, row)
                if j == 1:
                    ui_j = load_mat(ext, 18 * i, x, row + 1)
                else:
                    ui_j = mat_map(forward_z, ui)
                if i == 0:
                    uj_i = load_mat(ext, 18 * j, x + 1, row)
                else:
                    uj_i = load_mat(ext, 18 * j, x, row + 1)
                b = mat_mul(ui, uj_i)
                a = mat_mul(uj, ui_j)
                plaquette = anti_parts(mat_mul_dag(a, b))
                add(i, plaquette)
                add(j, plaquette, -1.0)
                low_i = anti_parts(mat_mul_dag(dag_mat_mul(uj, b), ui_j))
                low_j = anti_parts(mat_mul_dag(dag_mat_mul(ui, a), uj_i))
                if j == 2:
                    add(i, [backward_z(p) for p in low_i])
                for parts, shift, slot in ((low_i, j, 0), (low_j, i, 0 if j == 1 else 8)):
                    for n, p in enumerate(parts):
                        if shift == 0:
                            lx_ref[slot + n, x + 1, here, :] = p
                        elif shift == 1:
                            ly_ref[slot + n, x, row + 1 : row + 9, :] = p
                            if row:
                                rim_ref[x, slot + n : slot + n + 1, :] = p[7:8, :]
            for direction in range(3):
                for n in range(8):
                    gu_ref[8 * direction + n, x, here, :] = acc[direction][n]
        return 0

    lax.fori_loop(0, rows_x, step, 0)


def smear_kernel(fast, l_ref, gu_ref, lx_ref, ly_ref, rx_ref, ry_ref, table_ref, v_ref, s_ref, a0, a1, dz, pack):
    smear_sites(fast, l_ref, gu_ref, lx_ref, ly_ref, rx_ref, ry_ref, table_ref, v_ref, s_ref, a0, a1, dz, pack, lambda x: None)


def smear_sites(fast, l_ref, gu_ref, lx_ref, ly_ref, rx_ref, ry_ref, table_ref, v_ref, s_ref, a0, a1, dz, pack, arrive):
    rows_x, rows_y = v_ref.shape[1], v_ref.shape[2]

    def step(n_step, _):
        x = rows_x - 1 - n_step
        arrive(x)
        for row in (0, rows_y - 8):
            here = slice(row, row + 8)
            top = lax.broadcasted_iota(jnp.int32, (8, 128), 0) == 0

            def low_x(n):
                if rx_ref is None:
                    return lx_ref[n, x, here, :]
                return jnp.where(x == 0, rx_ref[n, here, :], lx_ref[n, x, here, :])

            def low_y(n):
                value = ly_ref[n, x, here, :]
                if row == 0:
                    value = jnp.where(top, ry_ref[x, n : n + 1, :], value)
                return value

            for direction in range(3):
                parts = []
                for n in range(8):
                    p = gu_ref[8 * direction + n, x, here, :]
                    if direction == 0:
                        p = p + low_y(n)
                    elif direction == 1:
                        p = p + low_x(n)
                    else:
                        p = p + low_x(8 + n) + low_y(8 + n)
                    parts.append(p)
                smeared = mat_mul(exp_parts(parts, SMEAR_RHO), load_mat(l_ref, 18 * direction, x, row))
                for r in range(3):
                    for c in range(3):
                        for part in range(2):
                            v_ref[18 * direction + 9 * part + 3 * r + c, x, here, :] = smeared[r][c][part]
                for n, p in enumerate(anti_parts(smeared)):
                    if direction == 0:
                        a0[n, x, here, :] = p
                    elif direction == 1:
                        a1[n, x, row + 1 : row + 9, :] = p
                    else:
                        dz[n, x, here, :] = p - backward_z(p)
        return 0

    lax.fori_loop(0, rows_x, step, 0)

    def divergence(n, _):
        pack[n] = jnp.zeros(pack.shape[1:], jnp.float32)
        for x in range(rows_x):
            total = a0[n, x] + dz[n, x] + a1[n, x, 1 : rows_y + 1, :]
            if x:
                total = total - a0[n, x - 1]
            lanes = slice(128 * (x // 2), 128 * (x // 2) + 128)
            pack[n, x % 2, 0:rows_y, lanes] = total
            pack[n, x % 2, 1:rows_y, lanes] = pack[n, x % 2, 1:rows_y, lanes] - a1[n, x, 1:rows_y, :]
            pack[n, x % 2, rows_y : rows_y + 1, lanes] = a1[n, x, rows_y : rows_y + 1, :]
        pack[n, 1, 0:rows_y, 128:256] = a0[n, rows_x - 1]
        return 0

    lax.fori_loop(0, 8, divergence, 0)
    if fast:
        out = jnp.dot(
            pack[...].reshape(256, 256), table_ref[...], precision=HIGHEST, preferred_element_type=jnp.float32
        )
        for half in range(2):
            s_ref[:, half] = out[:, 128 * half : 128 * half + 128].reshape(8, 2, 16, 128)
    else:
        s_ref[...] = pack[...]


def solve_kernel(r_ref, ty_ref, tyi_ref, cf_ref, ci_ref, f_ref, o_ref):
    half = lax.axis_index("gz")
    planes = []
    for gx in range(4):
        for xp in range(2):
            block = r_ref[4 * gx : 4 * gx + 4, xp].reshape(64, 128)
            planes.append(
                jnp.dot(ty_ref[...], block, precision=HIGHEST, preferred_element_type=jnp.float32)
            )
    turned = [pltpu.roll(p, 64, 1) for p in planes]
    modes = []
    for m in range(6):
        total = None
        for n in range(8):
            term = planes[n] * cf_ref[m, 2 * n : 2 * n + 1, :] + turned[n] * cf_ref[m, 2 * n + 1 : 2 * n + 2, :]
            total = term if total is None else total + term
        modes.append(total * f_ref[half, m])
    turned = [pltpu.roll(p, 64, 1) for p in modes]
    for gx in range(4):
        for xp in range(2):
            total = None
            for m in range(6):
                term = modes[m] * ci_ref[2 * gx + xp, 2 * m : 2 * m + 1, :] + turned[m] * ci_ref[2 * gx + xp, 2 * m + 1 : 2 * m + 2, :]
                total = term if total is None else total + term
            out = jnp.dot(tyi_ref[...], total, precision=HIGHEST, preferred_element_type=jnp.float32)
            o_ref[4 * gx : 4 * gx + 4, xp] = out.reshape(4, 16, 128)


def rotate_kernel(fast, q_ref, v_ref, table_ref, o_ref, acc, g, woven=False):
    rows_x, rows_y = v_ref.shape[1], v_ref.shape[2]
    if fast:
        left = jnp.concatenate([q_ref[:, 0].reshape(256, 128), q_ref[:, 1].reshape(256, 128)], axis=1)
        out = jnp.dot(left, table_ref[...], precision=HIGHEST, preferred_element_type=jnp.float32)
        for part in range(2):
            acc[:, 2 * part : 2 * part + 2] = out[:, 128 * part : 128 * part + 128].reshape(8, 2, 16, 128)
        src = acc
    else:
        src = q_ref

    def exponent(x, _):
        for row in (0, 8):
            here = slice(row, row + 8)
            m = exp_parts([src[n, x, here, :] for n in range(8)], HALF_STEP)
            for r in range(3):
                for c in range(3):
                    for part in range(2):
                        g[9 * part + 3 * r + c, x, here, :] = m[r][c][part]
        return 0

    lax.fori_loop(0, rows_x + 1, exponent, 0)

    def step(x, _):
        for row in (0, rows_y - 8):
            here = slice(row, row + 8)
            centre = load_mat(g, 0, x, row)
            for direction in range(3):
                if direction == 0:
                    other = load_mat(g, 0, x + 1, row)
                elif direction == 1:
                    other = load_mat(g, 0, x, row + 1)
                else:
                    other = mat_map(forward_z, centre)
                out = mat_mul_dag(mat_mul(centre, load_mat(v_ref, 18 * direction, x, row)), other)
                for r in range(3):
                    for c in range(3):
                        for part in range(2):
                            if woven:
                                rows = pl.ds(2 * row + part, 8, stride=2)
                                o_ref[9 * direction + 3 * r + c, x, rows, :] = out[r][c][part]
                            else:
                                o_ref[18 * direction + 9 * part + 3 * r + c, x, here, :] = out[r][c][part]
        return 0

    lax.fori_loop(0, rows_x, step, 0)


def neighbour(axis_sizes, step_x, step_y):
    n_x, n_y, n_z = axis_sizes
    gx = lax.axis_index("gx")
    block = lax.axis_index("gy") * n_z + lax.axis_index("gz")
    if step_x:
        return {"gx": lax.rem(gx + n_x + step_x, n_x)}
    block = lax.rem(block + n_y * n_z + step_y, n_y * n_z)
    return {"gy": lax.div(block, n_z), "gz": lax.rem(block, n_z)}


def exchange_kernel(sizes, way, pick, sx_ref, sy_ref, rx_ref, ry_ref, send, recv):
    barrier = pltpu.get_barrier_semaphore()
    for device in (neighbour(sizes, -way, 0), neighbour(sizes, 0, -way)):
        pl.semaphore_signal(barrier, inc=1, device_id=device, device_id_type=MESH)
    pl.semaphore_wait(barrier, 2)
    first, count, x = pick
    copies = []
    for n, (src, dst, device) in enumerate(
        (
            (sx_ref.at[pl.ds(first, count), x], rx_ref, neighbour(sizes, way, 0)),
            (sy_ref, ry_ref, neighbour(sizes, 0, way)),
        )
    ):
        copies.append(
            pltpu.make_async_remote_copy(
                src_ref=src,
                dst_ref=dst,
                send_sem=send.at[n],
                recv_sem=recv.at[n],
                device_id=device,
                device_id_type=MESH,
            )
        )
        copies[-1].start()
    for copy in copies:
        copy.wait()


def exchange(sizes, way, pick, key, sx, sy):
    shapes = (
        jax.ShapeDtypeStruct((pick[1],) + sx.shape[2:], jnp.float32),
        jax.ShapeDtypeStruct(sy.shape, jnp.float32),
    )
    return pl.pallas_call(
        functools.partial(exchange_kernel, sizes, way, pick),
        out_shape=shapes,
        in_specs=[ANY, ANY],
        out_specs=(ANY, ANY),
        scratch_shapes=[pltpu.SemaphoreType.DMA((2,)), pltpu.SemaphoreType.DMA((2,))],
        compiler_params=pltpu.CompilerParams(collective_id=key, has_side_effects=True),
    )(sx, sy)


def real_basis(length):
    x = np.arange(length)
    freq = np.zeros(length, np.int64)
    rows = np.zeros((length, length))
    rows[0] = 1.0 / math.sqrt(length)
    for n in range(1, length):
        k = (n + 1) // 2
        freq[n] = k
        angle = 2.0 * math.pi * ((k * x) % length) / length
        if 2 * k == length:
            rows[n] = np.cos(angle) / math.sqrt(length)
        else:
            rows[n] = (np.cos(angle) if n % 2 else np.sin(angle)) * math.sqrt(2.0 / length)
    return rows, 4.0 * np.sin(math.pi * freq / length) ** 2


def tables():
    tz, pz = real_basis(128)
    ty, py = real_basis(48)
    tx, px = real_basis(12)
    wide = np.zeros((2, 128, 2, 2, 64))
    for p in range(2):
        wide[p, :, :, p, :] = tz.T.reshape(128, 2, 64)
    wide = wide.reshape(256, 256)
    fy = np.zeros((48, 4, 16))
    iy = np.zeros((4, 16, 48))
    for b in range(4):
        fy[:, b, :12] = ty[:, 12 * b : 12 * b + 12]
        fy[:, b, 12] = -ty[:, (12 * b + 12) % 48]
        for r in range(13):
            iy[b, r] = ty[:, (12 * b + r) % 48]
    cf = np.zeros((6, 8, 2, 2, 64))
    ci = np.zeros((8, 6, 2, 2, 64))
    factor = np.zeros((2, 6, 48, 2, 64))
    for m in range(6):
        for q in range(2):
            squared = px[m + 6 * q] + py[None, :, None] + pz.reshape(2, 1, 64)
            factor[:, m, :, q] = np.where(squared > 1e-9, 12.0 / np.where(squared > 1e-9, squared, 1.0), 0.0)
            for gx in range(4):
                for xp in range(2):
                    for turn in range(2):
                        x = xp + 2 * (q if turn == 0 else 1 - q)
                        kx = m + 6 * q
                        site = (3 * gx + x) % 12
                        cf[m, 2 * gx + xp, turn, q] = -tx[kx, site] if x == 3 else tx[kx, site]
                        back = m + 6 * (q if turn == 0 else 1 - q)
                        ci[2 * gx + xp, m, turn, q] = tx[back, (3 * gx + xp + 2 * q) % 12]
    flat = lambda t, shape: jnp.asarray(t.reshape(shape), jnp.float32)
    return (
        flat(wide, (256, 256)),
        flat(wide.T.copy(), (256, 256)),
        flat(fy, (48, 64)),
        flat(iy, (64, 48)),
        flat(cf, (6, 16, 128)),
        flat(ci, (8, 12, 128)),
        flat(factor, (2, 6, 48, 128)),
    )


def local(kernel, shapes, scratch, *operands):
    single = isinstance(shapes[0], int)
    out = pl.pallas_call(
        kernel,
        out_shape=tuple(jax.ShapeDtypeStruct(s, jnp.float32) for s in ((shapes,) if single else shapes)),
        in_specs=[VMEM] * len(operands),
        out_specs=tuple(VMEM for _ in ((shapes,) if single else shapes)),
        scratch_shapes=[pltpu.VMEM(s, jnp.float32) for s in scratch],
        compiler_params=pltpu.CompilerParams(vmem_limit_bytes=40 << 20),
    )(*operands)
    return out[0] if single else out


def fused_kernel(sizes, *refs):
    l_ref, tables_hbm, o_ref = refs[0], refs[1:8], refs[8]
    tables_ref = refs[9:16]
    lv, hx, edge, hy, ext, gu, lx, ly, rim, ry, v, a0, a1, dz, pack, s, r, s2, q, acc, g = refs[16:37]
    send, recv, near = refs[37:]
    wide, wide_back, fy, iy, cf, ci, factor = tables_ref
    n_x, n_y, n_z = sizes
    total = n_x * n_y * n_z
    rows_x, rows_y = v.shape[1], v.shape[2]
    me = (lax.axis_index("gx") * n_y + lax.axis_index("gy")) * n_z + lax.axis_index("gz")

    def device(index):
        return {
            "gx": lax.div(index, n_y * n_z),
            "gy": lax.rem(lax.div(index, n_z), n_y),
            "gz": lax.rem(index, n_z),
        }

    pulls = [pltpu.make_async_copy(l_ref, lv, near.at[7])]
    pulls += [pltpu.make_async_copy(tables_hbm[n], tables_ref[n], near.at[n]) for n in range(7)]
    for pull in pulls:
        pull.start()
    barrier = pltpu.get_barrier_semaphore()
    for offset in range(1, total):
        pl.semaphore_signal(
            barrier, inc=1, device_id=device(lax.rem(me + offset, total)), device_id_type=MESH
        )
    started = []

    def push(slot, src, dst, target):
        copy = pltpu.make_async_remote_copy(
            src_ref=src,
            dst_ref=dst,
            send_sem=send.at[slot],
            recv_sem=recv.at[slot],
            device_id=target,
            device_id_type=MESH,
        )
        copy.start()
        started.append(copy)
        return copy

    pl.semaphore_wait(barrier, total - 1)
    face = push(0, l_ref.at[pl.ds(9, 18), 0], hx, neighbour(sizes, -1, 0))
    pulls[0].wait()
    for d in range(3):

        def fill(n, _):
            for part in range(2):
                ext[18 * d + 9 * part + n, 0:rows_x, 0:rows_y, :] = lv[
                    9 * d + n, :, pl.ds(part, rows_y, stride=2), :
                ]
            return 0

        if d == 1:
            continue
        lax.fori_loop(0, 9, fill, 0)
    for n in range(36):
        source = n if n < 18 else n + 18
        for x in range(rows_x):
            edge[x, n : n + 1, :] = ext[source, x, 0:1, :]
    line = push(1, edge, hy, neighbour(sizes, 0, -1))

    def fill_middle(n, _):
        for part in range(2):
            ext[18 + 9 * part + n, 0:rows_x, 0:rows_y, :] = lv[9 + n, :, pl.ds(part, rows_y, stride=2), :]
        return 0

    lax.fori_loop(0, 9, fill_middle, 0)
    line.wait_recv()
    for n in range(36):
        target = n if n < 18 else n + 18
        for x in range(rows_x):
            ext[target, x, rows_y : rows_y + 1, :] = hy[x, n : n + 1, :]

    def face_arrives(x):
        @pl.when(x == rows_x - 1)
        def _():
            face.wait_recv()

            def fill_face(n, _):
                for d in range(2):
                    for part in range(2):
                        ext[18 * d + 18 + 9 * part + n, rows_x, 0:rows_y, :] = hx[
                            9 * d + n, pl.ds(part, rows_y, stride=2), :
                        ]
                return 0

            lax.fori_loop(0, 9, fill_face, 0)

    staple_planes(ext, gu, lx, ly, rim, face_arrives)
    low_line = push(3, rim, ry, neighbour(sizes, 0, 1))
    low_face = push(2, lx.at[:, rows_x], lx.at[:, 0], neighbour(sizes, 1, 0))
    pulls[1].wait()
    low_line.wait_recv()

    def low_face_arrives(x):
        @pl.when(x == 0)
        def _():
            low_face.wait_recv()

    smear_sites(True, ext, gu, lx, ly, None, ry, wide, v, s, a0, a1, dz, pack, low_face_arrives)
    order = sorted(range(1, total), key=lambda o: -min(o, total - o))
    copies = []
    for offset in order:
        peer = lax.rem(me + offset, total)
        copies.append(push(3 + offset, s.at[lax.div(peer, 2), lax.rem(peer, 2)], r.at[me], device(peer)))
    r[me] = s[lax.div(me, 2), lax.rem(me, 2)]
    for pull in pulls[2:]:
        pull.wait()
    for copy in copies:
        copy.wait_recv()
    solve_kernel(r, fy, iy, cf, ci, factor, s2)
    copies = []
    for offset in order:
        peer = lax.rem(me + offset, total)
        copies.append(push(18 + offset, s2.at[peer], q.at[lax.div(me, 2), lax.rem(me, 2)], device(peer)))
    q[lax.div(me, 2), lax.rem(me, 2)] = s2[me]
    for copy in copies:
        copy.wait_recv()
    rotate_kernel(True, q, v, wide_back, o_ref, acc, g, woven=True)
    for copy in started:
        copy.wait_send()


def fused(sizes, gauge_links):
    rows_x, rows_y, depth = gauge_links.shape[4:]
    woven = jnp.transpose(gauge_links, (0, 2, 3, 4, 5, 1, 6)).reshape(27, rows_x, 2 * rows_y, depth)
    given = tables()
    shapes = [t.shape for t in given] + [
        woven.shape,
        (18, 2 * rows_y, depth),
        (rows_x, 36, depth),
        (rows_x, 36, depth),
        (54, rows_x + 1, 16, depth),
        (24, rows_x, rows_y, depth),
        (16, rows_x + 1, rows_y, depth),
        (16, rows_x, rows_y + 1, depth),
        (rows_x, 16, depth),
        (rows_x, 16, depth),
        (54, rows_x, rows_y, depth),
        (8, rows_x, rows_y, depth),
        (8, rows_x, rows_y + 1, depth),
        (8, rows_x, rows_y, depth),
        (8, 2, 16, 256),
        (8, 2, 2, 16, 128),
        (16, 2, 16, 128),
        (16, 2, 16, 128),
        (8, 2, 2, 16, 128),
        (8, 4, 16, 128),
        (18, rows_x + 1, 16, depth),
    ]
    out = pl.pallas_call(
        functools.partial(fused_kernel, sizes),
        out_shape=jax.ShapeDtypeStruct(woven.shape, jnp.float32),
        in_specs=[pl.BlockSpec(memory_space=pltpu.HBM)] * 8,
        out_specs=VMEM,
        scratch_shapes=[pltpu.VMEM(shape, jnp.float32) for shape in shapes]
        + [
            pltpu.SemaphoreType.DMA((34,)),
            pltpu.SemaphoreType.DMA((34,)),
            pltpu.SemaphoreType.DMA((8,)),
        ],
        compiler_params=pltpu.CompilerParams(
            collective_id=5, has_side_effects=True, vmem_limit_bytes=(64 << 20) - (1 << 19)
        ),
    )(woven, *given)
    return jnp.transpose(out.reshape(3, 3, 3, rows_x, rows_y, 2, depth), (0, 5, 1, 2, 3, 4, 6))


def shards(sizes, gauge_links):
    if sizes == (4, 2, 2):
        return fused(sizes, gauge_links)
    rows_x, rows_y, depth = gauge_links.shape[4:]
    wide, wide_back = tables()[:2]
    links = gauge_links.reshape(54, rows_x, rows_y, depth)
    first = links[:, :, 0, :]
    edge = jnp.moveaxis(jnp.concatenate([first[:18], first[36:]], axis=0), 0, 1)
    hx, hy = exchange(sizes, -1, (18, 36, 0), 1, links, edge)
    gu, lx, ly, rim = local(
        staple_kernel,
        (
            (24, rows_x, rows_y, depth),
            (16, rows_x + 1, rows_y, depth),
            (16, rows_x, rows_y + 1, depth),
            (rows_x, 16, depth),
        ),
        [(54, rows_x + 1, 16, depth)],
        links,
        hx,
        hy,
    )
    rx, ry = exchange(sizes, 1, (0, 16, rows_x), 2, lx, rim)
    smeared, blocks = local(
        functools.partial(smear_kernel, False),
        ((54, rows_x, rows_y, depth), (8, 2, 16, 256)),
        [
            (8, rows_x, rows_y, depth),
            (8, rows_x, rows_y + 1, depth),
            (8, rows_x, rows_y, depth),
            (8, 2, 16, 256),
        ],
        links,
        gu,
        lx,
        ly,
        rx,
        ry,
        wide,
    )
    used = blocks[:, :, : rows_y + 1]
    payload = jnp.concatenate([used[..., :depth], used[..., depth:]], axis=1)
    accel = general_solve(payload, rows_x, rows_y, depth)
    accel = jnp.pad(accel, ((0, 0), (0, 0), (0, 16 - accel.shape[2]), (0, 0)))
    rotated = local(
        functools.partial(rotate_kernel, False),
        (54, rows_x, rows_y, depth),
        [(8, 4, 16, 128), (18, rows_x + 1, 16, depth)],
        accel,
        smeared,
        wide_back,
    )
    return rotated.reshape(gauge_links.shape)


def solution(mesh):
    sizes = (mesh.shape["gx"], mesh.shape["gy"], mesh.shape["gz"])
    return jax.shard_map(
        functools.partial(shards, sizes),
        mesh=mesh,
        in_specs=(P(None, None, None, None, ("slices", "gx"), ("gy", "gz"), None),),
        out_specs=P(None, None, None, None, ("slices", "gx"), ("gy", "gz"), None),
        check_vma=False,
    )
```

```python
import functools
import math

import jax
import jax.numpy as jnp
import numpy as np
from jax import lax
from jax.experimental import pallas as pl
from jax.experimental.pallas import tpu as pltpu
from jax.sharding import PartitionSpec as P

SMEAR_RHO = 0.1
HALF_STEP = -0.04
MESH = pl.DeviceIdType.MESH
HIGHEST = lax.Precision.HIGHEST
VMEM = pl.BlockSpec(memory_space=pltpu.VMEM)
ANY = pl.BlockSpec(memory_space=pl.ANY)


def laplace_factor(freq_x, freq_y, freq_z, count_x, count_y, count_z):
    sine_x = jnp.sin(math.pi * freq_x / count_x)
    sine_y = jnp.sin(math.pi * freq_y / count_y)
    sine_z = jnp.sin(math.pi * freq_z / count_z)
    squared = (
        4.0 * (sine_x * sine_x)[:, None, None]
        + 4.0 * (sine_y * sine_y)[None, :, None]
        + 4.0 * (sine_z * sine_z)[None, None, :]
    )
    positive = squared > 0.0
    return jnp.where(positive, 12.0 / jnp.where(positive, squared, 1.0), 0.0)


def dft_tables(length):
    positions = jnp.arange(length, dtype=jnp.int32)
    phases = positions[:, None] * positions[None, :] % length
    angles = phases.astype(jnp.float32) * (2.0 * math.pi / length)
    return (jnp.cos(angles), jnp.sin(angles))


def transform(spectrum, axis_pos, direction_sign):
    length = spectrum.shape[axis_pos]
    cosine_table, sine_table = dft_tables(length)
    highest = lax.Precision.HIGHEST
    real_part = jnp.moveaxis(spectrum[0], axis_pos - 1, -1)
    imag_part = jnp.moveaxis(spectrum[1], axis_pos - 1, -1)
    out_real = jnp.dot(real_part, cosine_table, precision=highest) + direction_sign * jnp.dot(
        imag_part, sine_table, precision=highest
    )
    out_imag = jnp.dot(imag_part, cosine_table, precision=highest) - direction_sign * jnp.dot(
        real_part, sine_table, precision=highest
    )
    return jnp.moveaxis(jnp.stack([out_real, out_imag]), -1, axis_pos)


def general_solve(payload, rows_x, rows_y, depth_z):
    spectrum = jnp.stack([payload, jnp.zeros_like(payload)])
    fields_n = spectrum.shape[1]
    spectrum = transform(spectrum, 4, 1.0)
    spectrum = lax.all_to_all(spectrum, ("gy", "gz"), split_axis=4, concat_axis=3, tiled=True)
    groups_y = lax.axis_size(("gy", "gz"))
    span_z = spectrum.shape[4]
    blocks = spectrum.reshape((2, fields_n, rows_x + 1, groups_y, rows_y + 1, span_z))
    carried = jnp.roll(blocks[:, :, :, :, rows_y], 1, axis=3)
    first_row = blocks[:, :, :, :, 0] - carried
    blocks = jnp.concatenate([first_row[:, :, :, :, None], blocks[:, :, :, :, 1:rows_y]], axis=4)
    spectrum = blocks.reshape((2, fields_n, rows_x + 1, groups_y * rows_y, span_z))
    spectrum = transform(spectrum, 3, 1.0)
    spectrum = lax.all_to_all(spectrum, "gx", split_axis=3, concat_axis=2, tiled=True)
    groups_x = lax.axis_size("gx")
    span_y = spectrum.shape[3]
    blocks = spectrum.reshape((2, fields_n, groups_x, rows_x + 1, span_y, span_z))
    carried = jnp.roll(blocks[:, :, :, rows_x], 1, axis=2)
    first_row = blocks[:, :, :, 0] - carried
    blocks = jnp.concatenate([first_row[:, :, :, None], blocks[:, :, :, 1:rows_x]], axis=3)
    spectrum = blocks.reshape((2, fields_n, groups_x * rows_x, span_y, span_z))
    spectrum = transform(spectrum, 2, 1.0)
    length_x = groups_x * rows_x
    length_y = groups_y * rows_y
    freq_x = jnp.arange(length_x, dtype=jnp.float32)
    freq_y = (lax.axis_index("gx") * span_y + jnp.arange(span_y, dtype=jnp.int32)).astype(
        jnp.float32
    )
    freq_z = (lax.axis_index(("gy", "gz")) * span_z + jnp.arange(span_z, dtype=jnp.int32)).astype(
        jnp.float32
    )
    factor = laplace_factor(freq_x, freq_y, freq_z, length_x, length_y, depth_z) / float(
        length_x * length_y * depth_z
    )
    spectrum = spectrum * factor
    spectrum = transform(spectrum, 2, -1.0)
    blocks = spectrum.reshape((2, fields_n, groups_x, rows_x, span_y, span_z))
    following = jnp.roll(blocks[:, :, :, :1], -1, axis=2)
    spectrum = jnp.concatenate([blocks, following], axis=3).reshape(
        (2, fields_n, groups_x * (rows_x + 1), span_y, span_z)
    )
    spectrum = lax.all_to_all(spectrum, "gx", split_axis=2, concat_axis=3, tiled=True)
    spectrum = transform(spectrum, 3, -1.0)
    blocks = spectrum.reshape((2, fields_n, rows_x + 1, groups_y, rows_y, span_z))
    following = jnp.roll(blocks[:, :, :, :, :1], -1, axis=3)
    spectrum = jnp.concatenate([blocks, following], axis=4).reshape(
        (2, fields_n, rows_x + 1, groups_y * (rows_y + 1), span_z)
    )
    spectrum = lax.all_to_all(spectrum, ("gy", "gz"), split_axis=3, concat_axis=4, tiled=True)
    spectrum = transform(spectrum, 4, -1.0)
    return spectrum[0]


def cmul(a, b):
    return a[0] * b[0] - a[1] * b[1], a[0] * b[1] + a[1] * b[0]


def cadd(a, b):
    return a[0] + b[0], a[1] + b[1]


def conj(a):
    return a[0], -a[1]


def dot3(pairs):
    real = imag = None
    for a, b, flip_a, flip_b in pairs:
        rr, ii = a[0] * b[0], a[1] * b[1]
        ri, ir = a[0] * b[1], a[1] * b[0]
        r = rr - ii if flip_a == flip_b else rr + ii
        i = {(0, 0): lambda: ri + ir, (0, 1): lambda: ir - ri, (1, 0): lambda: ri - ir}[(flip_a, flip_b)]()
        real = r if real is None else real + r
        imag = i if imag is None else imag + i
    return real, imag


def mat_mul(a, b):
    return [[dot3([(a[r][m], b[m][c], 0, 0) for m in range(3)]) for c in range(3)] for r in range(3)]


def mat_mul_dag(a, b):
    return [[dot3([(a[r][m], b[c][m], 0, 1) for m in range(3)]) for c in range(3)] for r in range(3)]


def dag_mat_mul(a, b):
    return [[dot3([(a[m][r], b[m][c], 1, 0) for m in range(3)]) for c in range(3)] for r in range(3)]


def anti_parts(m):
    third = (m[0][0][1] + m[1][1][1] + m[2][2][1]) * (1.0 / 3.0)
    out = [m[0][0][1] - third, m[1][1][1] - third]
    for r, c in ((0, 1), (0, 2), (1, 2)):
        out.append(0.5 * (m[r][c][0] - m[c][r][0]))
        out.append(0.5 * (m[r][c][1] + m[c][r][1]))
    return out


def exp_parts(parts, scale):
    v = [0.5 * scale * p for p in parts]
    h0, h1 = v[0], v[1]
    h2 = -h0 - h1
    h01, h02, h12 = (v[3], -v[2]), (v[5], -v[4]), (v[7], -v[6])
    n01, n02, n12 = [h[0] * h[0] + h[1] * h[1] for h in (h01, h02, h12)]
    s0, s1, s2 = h0 * h0, h1 * h1, h2 * h2
    k00, k11, k22 = s0 + n01 + n02, s1 + n01 + n12, s2 + n02 + n12
    p02 = cmul(h01, h12)
    q = cmul(h02, conj(h12))
    w = cmul(conj(h01), h02)
    k01 = (q[0] - h2 * h01[0], q[1] - h2 * h01[1])
    k02 = (p02[0] - h1 * h02[0], p02[1] - h1 * h02[1])
    k12 = (w[0] - h0 * h12[0], w[1] - h0 * h12[1])
    t = 0.5 * (k00 + k11 + k22)
    d = h0 * h1 * h2 + 2.0 * (p02[0] * h02[0] + p02[1] * h02[1]) - h0 * n12 - h1 * n02 - h2 * n01
    t2 = t * t
    q0 = (1.0 - d * d * (1.0 / 720.0), d * (t * (1.0 / 120.0) - 1.0 / 6.0))
    q1 = (d * (1.0 / 24.0 - t * (1.0 / 360.0)), 1.0 - t * (1.0 / 6.0) + t2 * (1.0 / 120.0))
    q2 = (t * (1.0 / 24.0) - 0.5 - t2 * (1.0 / 720.0), d * (1.0 / 120.0))
    q00, q01, q02, q11, q12, q22 = cmul(q0, q0), cmul(q0, q1), cmul(q0, q2), cmul(q1, q1), cmul(q1, q2), cmul(q2, q2)
    e0 = [q00[n] + 2.0 * d * q12[n] for n in range(2)]
    e1 = [2.0 * (q01[n] + t * q12[n]) + d * q22[n] for n in range(2)]
    e2 = [2.0 * q02[n] + q11[n] + t * q22[n] for n in range(2)]
    out = [[None] * 3 for _ in range(3)]
    for r, (h, k) in enumerate(((h0, k00), (h1, k11), (h2, k22))):
        out[r][r] = (e0[0] + e1[0] * h + e2[0] * k, e0[1] + e1[1] * h + e2[1] * k)
    for r, c, h, k in ((0, 1, h01, k01), (0, 2, h02, k02), (1, 2, h12, k12)):
        out[r][c] = cadd(cmul(e1, h), cmul(e2, k))
        out[c][r] = cadd(cmul(e1, conj(h)), cmul(e2, conj(k)))
    return out


def mat_map(fn, m):
    return [[(fn(e[0]), fn(e[1])) for e in row] for row in m]


def load_mat(ref, base, x, row):
    return [
        [tuple(ref[base + 9 * part + 3 * r + c, x, row : row + 8, :] for part in range(2)) for c in range(3)]
        for r in range(3)
    ]


def forward_z(value):
    return pltpu.roll(value, value.shape[1] - 1, 1)


def backward_z(value):
    return pltpu.roll(value, 1, 1)


def staple_kernel(l_ref, hx_ref, hy_ref, gu_ref, lx_ref, ly_ref, rim_ref, ext):
    rows_x, rows_y = l_ref.shape[1], l_ref.shape[2]

    def fill(n, _):
        ext[n, 0:rows_x, 0:rows_y, :] = l_ref[n]
        return 0

    lax.fori_loop(0, 54, fill, 0)

    def fill_x(n, _):
        ext[18 + n, rows_x, 0:rows_y, :] = hx_ref[n]
        return 0

    lax.fori_loop(0, 36, fill_x, 0)
    for n in range(36):
        target = n if n < 18 else n + 18
        for x in range(rows_x):
            ext[target, x, rows_y : rows_y + 1, :] = hy_ref[x, n : n + 1, :]
    staple_planes(ext, gu_ref, lx_ref, ly_ref, rim_ref, lambda x: None)


def staple_planes(ext, gu_ref, lx_ref, ly_ref, rim_ref, arrive):
    rows_x, rows_y = gu_ref.shape[1], gu_ref.shape[2]

    def step(x, _):
        arrive(x)
        for row in (0, rows_y - 8):
            here = slice(row, row + 8)
            acc = [None] * 3

            def add(direction, parts, sign=1.0):
                if acc[direction] is None:
                    acc[direction] = parts if sign > 0 else [-p for p in parts]
                elif sign > 0:
                    acc[direction] = [p + q for p, q in zip(acc[direction], parts)]
                else:
                    acc[direction] = [p - q for p, q in zip(acc[direction], parts)]

            for i, j in ((0, 1), (0, 2), (1, 2)):
                ui, uj = load_mat(ext, 18 * i, x, row), load_mat(ext, 18 * j, x, row)
                if j == 1:
                    ui_j = load_mat(ext, 18 * i, x, row + 1)
                else:
                    ui_j = mat_map(forward_z, ui)
                if i == 0:
                    uj_i = load_mat(ext, 18 * j, x + 1, row)
                else:
                    uj_i = load_mat(ext, 18 * j, x, row + 1)
                b = mat_mul(ui, uj_i)
                a = mat_mul(uj, ui_j)
                plaquette = anti_parts(mat_mul_dag(a, b))
                add(i, plaquette)
                add(j, plaquette, -1.0)
                low_i = anti_parts(mat_mul_dag(dag_mat_mul(uj, b), ui_j))
                low_j = anti_parts(mat_mul_dag(dag_mat_mul(ui, a), uj_i))
                if j == 2:
                    add(i, [backward_z(p) for p in low_i])
                for parts, shift, slot in ((low_i, j, 0), (low_j, i, 0 if j == 1 else 8)):
                    for n, p in enumerate(parts):
                        if shift == 0:
                            lx_ref[slot + n, x + 1, here, :] = p
                        elif shift == 1:
                            ly_ref[slot + n, x, row + 1 : row + 9, :] = p
                            if row:
                                rim_ref[x, slot + n : slot + n + 1, :] = p[7:8, :]
            for direction in range(3):
                for n in range(8):
                    gu_ref[8 * direction + n, x, here, :] = acc[direction][n]
        return 0

    lax.fori_loop(0, rows_x, step, 0)


def smear_kernel(fast, l_ref, gu_ref, lx_ref, ly_ref, rx_ref, ry_ref, table_ref, v_ref, s_ref, a0, a1, dz, pack):
    smear_sites(fast, l_ref, gu_ref, lx_ref, ly_ref, rx_ref, ry_ref, table_ref, v_ref, s_ref, a0, a1, dz, pack, lambda x: None)


def smear_sites(fast, l_ref, gu_ref, lx_ref, ly_ref, rx_ref, ry_ref, table_ref, v_ref, s_ref, a0, a1, dz, pack, arrive):
    rows_x, rows_y = v_ref.shape[1], v_ref.shape[2]

    def step(n_step, _):
        x = rows_x - 1 - n_step
        arrive(x)
        for row in (0, rows_y - 8):
            here = slice(row, row + 8)
            top = lax.broadcasted_iota(jnp.int32, (8, 128), 0) == 0

            def low_x(n):
                if rx_ref is None:
                    return lx_ref[n, x, here, :]
                return jnp.where(x == 0, rx_ref[n, here, :], lx_ref[n, x, here, :])

            def low_y(n):
                value = ly_ref[n, x, here, :]
                if row == 0:
                    value = jnp.where(top, ry_ref[x, n : n + 1, :], value)
                return value

            for direction in range(3):
                parts = []
                for n in range(8):
                    p = gu_ref[8 * direction + n, x, here, :]
                    if direction == 0:
                        p = p + low_y(n)
                    elif direction == 1:
                        p = p + low_x(n)
                    else:
                        p = p + low_x(8 + n) + low_y(8 + n)
                    parts.append(p)
                smeared = mat_mul(exp_parts(parts, SMEAR_RHO), load_mat(l_ref, 18 * direction, x, row))
                for r in range(3):
                    for c in range(3):
                        for part in range(2):
                            v_ref[18 * direction + 9 * part + 3 * r + c, x, here, :] = smeared[r][c][part]
                for n, p in enumerate(anti_parts(smeared)):
                    if direction == 0:
                        a0[n, x, here, :] = p
                    elif direction == 1:
                        a1[n, x, row + 1 : row + 9, :] = p
                    else:
                        dz[n, x, here, :] = p - backward_z(p)
        return 0

    lax.fori_loop(0, rows_x, step, 0)

    def divergence(n, _):
        pack[n] = jnp.zeros(pack.shape[1:], jnp.float32)
        for x in range(rows_x):
            total = a0[n, x] + dz[n, x] + a1[n, x, 1 : rows_y + 1, :]
            if x:
                total = total - a0[n, x - 1]
            lanes = slice(128 * (x // 2), 128 * (x // 2) + 128)
            pack[n, x % 2, 0:rows_y, lanes] = total
            pack[n, x % 2, 1:rows_y, lanes] = pack[n, x % 2, 1:rows_y, lanes] - a1[n, x, 1:rows_y, :]
            pack[n, x % 2, rows_y : rows_y + 1, lanes] = a1[n, x, rows_y : rows_y + 1, :]
        pack[n, 1, 0:rows_y, 128:256] = a0[n, rows_x - 1]
        return 0

    lax.fori_loop(0, 8, divergence, 0)
    if fast:
        out = jnp.dot(
            pack[...].reshape(256, 256), table_ref[...], precision=HIGHEST, preferred_element_type=jnp.float32
        )
        for half in range(2):
            s_ref[:, half] = out[:, 128 * half : 128 * half + 128].reshape(8, 2, 16, 128)
    else:
        s_ref[...] = pack[...]


def solve_blocks(r_ref, ty_ref, tyi_ref, cf_ref, ci_ref, f_ref, o_ref, ready, done):
    half = lax.axis_index("gz")
    mine = lax.axis_index("gx")
    modes = [None] * 6
    for k in (0, 1, 3, 2):
        ready(k)
        gx = lax.rem(mine + 4 - k, 4)
        for xp in range(2):
            block = r_ref[pl.ds(4 * gx, 4), xp].reshape(64, 128)
            plane = jnp.dot(ty_ref[...], block, precision=HIGHEST, preferred_element_type=jnp.float32)
            turned = pltpu.roll(plane, 64, 1)
            for m in range(6):
                term = (
                    plane * cf_ref[2 * gx + xp, 2 * m : 2 * m + 1, :]
                    + turned * cf_ref[2 * gx + xp, 2 * m + 1 : 2 * m + 2, :]
                )
                modes[m] = term if modes[m] is None else modes[m] + term
    modes = [modes[m] * f_ref[half, m] for m in range(6)]
    turned = [pltpu.roll(p, 64, 1) for p in modes]
    for k in (2, 1, 3, 0):
        gx = lax.rem(mine + k, 4)
        for xp in range(2):
            total = None
            for m in range(6):
                term = (
                    modes[m] * ci_ref[2 * gx + xp, 2 * m : 2 * m + 1, :]
                    + turned[m] * ci_ref[2 * gx + xp, 2 * m + 1 : 2 * m + 2, :]
                )
                total = term if total is None else total + term
            out = jnp.dot(tyi_ref[...], total, precision=HIGHEST, preferred_element_type=jnp.float32)
            o_ref[pl.ds(4 * gx, 4), xp] = out.reshape(4, 16, 128)
        done(k)


def rotate_kernel(fast, q_ref, v_ref, table_ref, o_ref, acc, g, woven=False):
    rows_x, rows_y = v_ref.shape[1], v_ref.shape[2]
    if fast:
        left = jnp.concatenate([q_ref[:, 0].reshape(256, 128), q_ref[:, 1].reshape(256, 128)], axis=1)
        out = jnp.dot(left, table_ref[...], precision=HIGHEST, preferred_element_type=jnp.float32)
        for part in range(2):
            acc[:, 2 * part : 2 * part + 2] = out[:, 128 * part : 128 * part + 128].reshape(8, 2, 16, 128)
        src = acc
    else:
        src = q_ref

    def exponent(x, _):
        for row in (0, 8):
            here = slice(row, row + 8)
            m = exp_parts([src[n, x, here, :] for n in range(8)], HALF_STEP)
            for r in range(3):
                for c in range(3):
                    for part in range(2):
                        g[9 * part + 3 * r + c, x, here, :] = m[r][c][part]
        return 0

    lax.fori_loop(0, rows_x + 1, exponent, 0)

    def step(x, _):
        for row in (0, rows_y - 8):
            here = slice(row, row + 8)
            centre = load_mat(g, 0, x, row)
            for direction in range(3):
                if direction == 0:
                    other = load_mat(g, 0, x + 1, row)
                elif direction == 1:
                    other = load_mat(g, 0, x, row + 1)
                else:
                    other = mat_map(forward_z, centre)
                out = mat_mul_dag(mat_mul(centre, load_mat(v_ref, 18 * direction, x, row)), other)
                for r in range(3):
                    for c in range(3):
                        for part in range(2):
                            if woven:
                                rows = pl.ds(2 * row + part, 8, stride=2)
                                o_ref[9 * direction + 3 * r + c, x, rows, :] = out[r][c][part]
                            else:
                                o_ref[18 * direction + 9 * part + 3 * r + c, x, here, :] = out[r][c][part]
        return 0

    lax.fori_loop(0, rows_x, step, 0)


def neighbour(axis_sizes, step_x, step_y):
    n_x, n_y, n_z = axis_sizes
    gx = lax.axis_index("gx")
    block = lax.axis_index("gy") * n_z + lax.axis_index("gz")
    if step_x:
        return {"gx": lax.rem(gx + n_x + step_x, n_x)}
    block = lax.rem(block + n_y * n_z + step_y, n_y * n_z)
    return {"gy": lax.div(block, n_z), "gz": lax.rem(block, n_z)}


def exchange_kernel(sizes, way, pick, sx_ref, sy_ref, rx_ref, ry_ref, send, recv):
    barrier = pltpu.get_barrier_semaphore()
    for device in (neighbour(sizes, -way, 0), neighbour(sizes, 0, -way)):
        pl.semaphore_signal(barrier, inc=1, device_id=device, device_id_type=MESH)
    pl.semaphore_wait(barrier, 2)
    first, count, x = pick
    copies = []
    for n, (src, dst, device) in enumerate(
        (
            (sx_ref.at[pl.ds(first, count), x], rx_ref, neighbour(sizes, way, 0)),
            (sy_ref, ry_ref, neighbour(sizes, 0, way)),
        )
    ):
        copies.append(
            pltpu.make_async_remote_copy(
                src_ref=src,
                dst_ref=dst,
                send_sem=send.at[n],
                recv_sem=recv.at[n],
                device_id=device,
                device_id_type=MESH,
            )
        )
        copies[-1].start()
    for copy in copies:
        copy.wait()


def exchange(sizes, way, pick, key, sx, sy):
    shapes = (
        jax.ShapeDtypeStruct((pick[1],) + sx.shape[2:], jnp.float32),
        jax.ShapeDtypeStruct(sy.shape, jnp.float32),
    )
    return pl.pallas_call(
        functools.partial(exchange_kernel, sizes, way, pick),
        out_shape=shapes,
        in_specs=[ANY, ANY],
        out_specs=(ANY, ANY),
        scratch_shapes=[pltpu.SemaphoreType.DMA((2,)), pltpu.SemaphoreType.DMA((2,))],
        compiler_params=pltpu.CompilerParams(collective_id=key, has_side_effects=True),
    )(sx, sy)


def real_basis(length):
    x = np.arange(length)
    freq = np.zeros(length, np.int64)
    rows = np.zeros((length, length))
    rows[0] = 1.0 / math.sqrt(length)
    for n in range(1, length):
        k = (n + 1) // 2
        freq[n] = k
        angle = 2.0 * math.pi * ((k * x) % length) / length
        if 2 * k == length:
            rows[n] = np.cos(angle) / math.sqrt(length)
        else:
            rows[n] = (np.cos(angle) if n % 2 else np.sin(angle)) * math.sqrt(2.0 / length)
    return rows, 4.0 * np.sin(math.pi * freq / length) ** 2


def tables():
    tz, pz = real_basis(128)
    ty, py = real_basis(48)
    tx, px = real_basis(12)
    wide = np.zeros((2, 128, 2, 2, 64))
    for p in range(2):
        wide[p, :, :, p, :] = tz.T.reshape(128, 2, 64)
    wide = wide.reshape(256, 256)
    fy = np.zeros((48, 4, 16))
    iy = np.zeros((4, 16, 48))
    for b in range(4):
        fy[:, b, :12] = ty[:, 12 * b : 12 * b + 12]
        fy[:, b, 12] = -ty[:, (12 * b + 12) % 48]
        for r in range(13):
            iy[b, r] = ty[:, (12 * b + r) % 48]
    cf = np.zeros((8, 6, 2, 2, 64))
    ci = np.zeros((8, 6, 2, 2, 64))
    factor = np.zeros((2, 6, 48, 2, 64))
    for m in range(6):
        for q in range(2):
            squared = px[m + 6 * q] + py[None, :, None] + pz.reshape(2, 1, 64)
            factor[:, m, :, q] = np.where(squared > 1e-9, 12.0 / np.where(squared > 1e-9, squared, 1.0), 0.0)
            for gx in range(4):
                for xp in range(2):
                    for turn in range(2):
                        x = xp + 2 * (q if turn == 0 else 1 - q)
                        kx = m + 6 * q
                        site = (3 * gx + x) % 12
                        cf[2 * gx + xp, m, turn, q] = -tx[kx, site] if x == 3 else tx[kx, site]
                        back = m + 6 * (q if turn == 0 else 1 - q)
                        ci[2 * gx + xp, m, turn, q] = tx[back, (3 * gx + xp + 2 * q) % 12]
    flat = lambda t, shape: jnp.asarray(t.reshape(shape), jnp.float32)
    return (
        flat(wide, (256, 256)),
        flat(wide.T.copy(), (256, 256)),
        flat(fy, (48, 64)),
        flat(iy, (64, 48)),
        flat(cf, (8, 12, 128)),
        flat(ci, (8, 12, 128)),
        flat(factor, (2, 6, 48, 128)),
    )


def local(kernel, shapes, scratch, *operands):
    single = isinstance(shapes[0], int)
    out = pl.pallas_call(
        kernel,
        out_shape=tuple(jax.ShapeDtypeStruct(s, jnp.float32) for s in ((shapes,) if single else shapes)),
        in_specs=[VMEM] * len(operands),
        out_specs=tuple(VMEM for _ in ((shapes,) if single else shapes)),
        scratch_shapes=[pltpu.VMEM(s, jnp.float32) for s in scratch],
        compiler_params=pltpu.CompilerParams(vmem_limit_bytes=40 << 20),
    )(*operands)
    return out[0] if single else out


def fused_kernel(sizes, *refs):
    l_ref, tables_hbm, o_ref = refs[0], refs[1:8], refs[8]
    tables_ref = refs[9:16]
    lv, hx, edge, hy, ext, gu, lx, ly, rim, ry, v, a0, a1, dz, pack, s, r, s2, q, acc, g = refs[16:37]
    send, recv, near = refs[37:]
    wide, wide_back, fy, iy, cf, ci, factor = tables_ref
    n_x, n_y, n_z = sizes
    total = n_x * n_y * n_z
    rows_x, rows_y = v.shape[1], v.shape[2]
    me = (lax.axis_index("gx") * n_y + lax.axis_index("gy")) * n_z + lax.axis_index("gz")

    def device(index):
        return {
            "gx": lax.div(index, n_y * n_z),
            "gy": lax.rem(lax.div(index, n_z), n_y),
            "gz": lax.rem(index, n_z),
        }

    pulls = [pltpu.make_async_copy(l_ref, lv, near.at[7])]
    pulls += [pltpu.make_async_copy(tables_hbm[n], tables_ref[n], near.at[n]) for n in range(7)]
    for pull in pulls:
        pull.start()
    r[...] = jnp.zeros(r.shape, jnp.float32)
    barrier = pltpu.get_barrier_semaphore()
    for offset in range(1, total):
        pl.semaphore_signal(
            barrier, inc=1, device_id=device(lax.rem(me + offset, total)), device_id_type=MESH
        )
    started = []

    def push(slot, src, dst, target):
        copy = pltpu.make_async_remote_copy(
            src_ref=src,
            dst_ref=dst,
            send_sem=send.at[slot],
            recv_sem=recv.at[slot],
            device_id=target,
            device_id_type=MESH,
        )
        copy.start()
        started.append(copy)
        return copy

    pl.semaphore_wait(barrier, total - 1)
    face = push(0, l_ref.at[pl.ds(9, 18), 0], hx, neighbour(sizes, -1, 0))
    pulls[0].wait()
    for d in range(3):

        def fill(n, _):
            for part in range(2):
                ext[18 * d + 9 * part + n, 0:rows_x, 0:rows_y, :] = lv[
                    9 * d + n, :, pl.ds(part, rows_y, stride=2), :
                ]
            return 0

        if d == 1:
            continue
        lax.fori_loop(0, 9, fill, 0)
    for n in range(36):
        source = n if n < 18 else n + 18
        for x in range(rows_x):
            edge[x, n : n + 1, :] = ext[source, x, 0:1, :]
    line = push(1, edge, hy, neighbour(sizes, 0, -1))

    def fill_middle(n, _):
        for part in range(2):
            ext[18 + 9 * part + n, 0:rows_x, 0:rows_y, :] = lv[9 + n, :, pl.ds(part, rows_y, stride=2), :]
        return 0

    lax.fori_loop(0, 9, fill_middle, 0)
    line.wait_recv()
    for n in range(36):
        target = n if n < 18 else n + 18
        for x in range(rows_x):
            ext[target, x, rows_y : rows_y + 1, :] = hy[x, n : n + 1, :]

    def face_arrives(x):
        @pl.when(x == rows_x - 1)
        def _():
            face.wait_recv()

            def fill_face(n, _):
                for d in range(2):
                    for part in range(2):
                        ext[18 * d + 18 + 9 * part + n, rows_x, 0:rows_y, :] = hx[
                            9 * d + n, pl.ds(part, rows_y, stride=2), :
                        ]
                return 0

            lax.fori_loop(0, 9, fill_face, 0)

    staple_planes(ext, gu, lx, ly, rim, face_arrives)
    low_line = push(3, rim, ry, neighbour(sizes, 0, 1))
    low_face = push(2, lx.at[:, rows_x], lx.at[:, 0], neighbour(sizes, 1, 0))
    pulls[1].wait()
    low_line.wait_recv()

    def low_face_arrives(x):
        @pl.when(x == 0)
        def _():
            low_face.wait_recv()

    smear_sites(True, ext, gu, lx, ly, None, ry, wide, v, s, a0, a1, dz, pack, low_face_arrives)
    used = rows_y + 1
    mine, spot = lax.div(me, 4), lax.rem(me, 4)
    there, back = {}, {}

    def partner(k, j):
        return 4 * lax.rem(mine + k, 4) + lax.rem(spot + j, 4)

    for k in (2, 1, 3, 0):
        for j in range(4):
            if k or j:
                peer = partner(k, j)
                there[k, j] = push(
                    3 + 4 * k + j,
                    s.at[lax.div(peer, 2), lax.rem(peer, 2), :, pl.ds(0, used)],
                    r.at[me, :, pl.ds(0, used)],
                    device(peer),
                )
    r[me, :, 0:used, :] = s[lax.div(me, 2), lax.rem(me, 2), :, 0:used, :]
    for pull in pulls[2:]:
        pull.wait()

    def ready(k):
        for j in range(4):
            if k or j:
                there[k, j].wait_recv()

    def done(k):
        for j in range(4):
            if k or j:
                peer = partner(k, j)
                back[k, j] = push(
                    18 + 4 * k + j,
                    s2.at[peer, :, pl.ds(0, used)],
                    q.at[lax.div(me, 2), lax.rem(me, 2), :, pl.ds(0, used)],
                    device(peer),
                )

    solve_blocks(r, fy, iy, cf, ci, factor, s2, ready, done)
    q[lax.div(me, 2), lax.rem(me, 2), :, 0:used, :] = s2[me, :, 0:used, :]
    for copy in back.values():
        copy.wait_recv()
    rotate_kernel(True, q, v, wide_back, o_ref, acc, g, woven=True)
    for copy in started:
        copy.wait_send()


def fused(sizes, gauge_links):
    rows_x, rows_y, depth = gauge_links.shape[4:]
    woven = jnp.transpose(gauge_links, (0, 2, 3, 4, 5, 1, 6)).reshape(27, rows_x, 2 * rows_y, depth)
    given = tables()
    shapes = [t.shape for t in given] + [
        woven.shape,
        (18, 2 * rows_y, depth),
        (rows_x, 36, depth),
        (rows_x, 36, depth),
        (54, rows_x + 1, 16, depth),
        (24, rows_x, rows_y, depth),
        (16, rows_x + 1, rows_y, depth),
        (16, rows_x, rows_y + 1, depth),
        (rows_x, 16, depth),
        (rows_x, 16, depth),
        (54, rows_x, rows_y, depth),
        (8, rows_x, rows_y, depth),
        (8, rows_x, rows_y + 1, depth),
        (8, rows_x, rows_y, depth),
        (8, 2, 16, 256),
        (8, 2, 2, 16, 128),
        (16, 2, 16, 128),
        (16, 2, 16, 128),
        (8, 2, 2, 16, 128),
        (8, 4, 16, 128),
        (18, rows_x + 1, 16, depth),
    ]
    out = pl.pallas_call(
        functools.partial(fused_kernel, sizes),
        out_shape=jax.ShapeDtypeStruct(woven.shape, jnp.float32),
        in_specs=[pl.BlockSpec(memory_space=pltpu.HBM)] * 8,
        out_specs=VMEM,
        scratch_shapes=[pltpu.VMEM(shape, jnp.float32) for shape in shapes]
        + [
            pltpu.SemaphoreType.DMA((34,)),
            pltpu.SemaphoreType.DMA((34,)),
            pltpu.SemaphoreType.DMA((8,)),
        ],
        compiler_params=pltpu.CompilerParams(
            collective_id=5, has_side_effects=True, vmem_limit_bytes=(64 << 20) - (1 << 19)
        ),
    )(woven, *given)
    return jnp.transpose(out.reshape(3, 3, 3, rows_x, rows_y, 2, depth), (0, 5, 1, 2, 3, 4, 6))


def shards(sizes, gauge_links):
    if sizes == (4, 2, 2):
        return fused(sizes, gauge_links)
    rows_x, rows_y, depth = gauge_links.shape[4:]
    wide, wide_back = tables()[:2]
    links = gauge_links.reshape(54, rows_x, rows_y, depth)
    first = links[:, :, 0, :]
    edge = jnp.moveaxis(jnp.concatenate([first[:18], first[36:]], axis=0), 0, 1)
    hx, hy = exchange(sizes, -1, (18, 36, 0), 1, links, edge)
    gu, lx, ly, rim = local(
        staple_kernel,
        (
            (24, rows_x, rows_y, depth),
            (16, rows_x + 1, rows_y, depth),
            (16, rows_x, rows_y + 1, depth),
            (rows_x, 16, depth),
        ),
        [(54, rows_x + 1, 16, depth)],
        links,
        hx,
        hy,
    )
    rx, ry = exchange(sizes, 1, (0, 16, rows_x), 2, lx, rim)
    smeared, blocks = local(
        functools.partial(smear_kernel, False),
        ((54, rows_x, rows_y, depth), (8, 2, 16, 256)),
        [
            (8, rows_x, rows_y, depth),
            (8, rows_x, rows_y + 1, depth),
            (8, rows_x, rows_y, depth),
            (8, 2, 16, 256),
        ],
        links,
        gu,
        lx,
        ly,
        rx,
        ry,
        wide,
    )
    used = blocks[:, :, : rows_y + 1]
    payload = jnp.concatenate([used[..., :depth], used[..., depth:]], axis=1)
    accel = general_solve(payload, rows_x, rows_y, depth)
    accel = jnp.pad(accel, ((0, 0), (0, 0), (0, 16 - accel.shape[2]), (0, 0)))
    rotated = local(
        functools.partial(rotate_kernel, False),
        (54, rows_x, rows_y, depth),
        [(8, 4, 16, 128), (18, rows_x + 1, 16, depth)],
        accel,
        smeared,
        wide_back,
    )
    return rotated.reshape(gauge_links.shape)


def solution(mesh):
    sizes = (mesh.shape["gx"], mesh.shape["gy"], mesh.shape["gz"])
    return jax.shard_map(
        functools.partial(shards, sizes),
        mesh=mesh,
        in_specs=(P(None, None, None, None, ("slices", "gx"), ("gy", "gz"), None),),
        out_specs=P(None, None, None, None, ("slices", "gx"), ("gy", "gz"), None),
        check_vma=False,
    )
```

```python
import functools
import math

import jax
import jax.numpy as jnp
import numpy as np
from jax import lax
from jax.experimental import pallas as pl
from jax.experimental.pallas import tpu as pltpu
from jax.sharding import PartitionSpec as P

SMEAR_RHO = 0.1
HALF_STEP = -0.04
MESH = pl.DeviceIdType.MESH
HIGHEST = lax.Precision.HIGHEST
VMEM = pl.BlockSpec(memory_space=pltpu.VMEM)
ANY = pl.BlockSpec(memory_space=pl.ANY)


def laplace_factor(freq_x, freq_y, freq_z, count_x, count_y, count_z):
    sine_x = jnp.sin(math.pi * freq_x / count_x)
    sine_y = jnp.sin(math.pi * freq_y / count_y)
    sine_z = jnp.sin(math.pi * freq_z / count_z)
    squared = (
        4.0 * (sine_x * sine_x)[:, None, None]
        + 4.0 * (sine_y * sine_y)[None, :, None]
        + 4.0 * (sine_z * sine_z)[None, None, :]
    )
    positive = squared > 0.0
    return jnp.where(positive, 12.0 / jnp.where(positive, squared, 1.0), 0.0)


def dft_tables(length):
    positions = jnp.arange(length, dtype=jnp.int32)
    phases = positions[:, None] * positions[None, :] % length
    angles = phases.astype(jnp.float32) * (2.0 * math.pi / length)
    return (jnp.cos(angles), jnp.sin(angles))


def transform(spectrum, axis_pos, direction_sign):
    length = spectrum.shape[axis_pos]
    cosine_table, sine_table = dft_tables(length)
    highest = lax.Precision.HIGHEST
    real_part = jnp.moveaxis(spectrum[0], axis_pos - 1, -1)
    imag_part = jnp.moveaxis(spectrum[1], axis_pos - 1, -1)
    out_real = jnp.dot(real_part, cosine_table, precision=highest) + direction_sign * jnp.dot(
        imag_part, sine_table, precision=highest
    )
    out_imag = jnp.dot(imag_part, cosine_table, precision=highest) - direction_sign * jnp.dot(
        real_part, sine_table, precision=highest
    )
    return jnp.moveaxis(jnp.stack([out_real, out_imag]), -1, axis_pos)


def general_solve(payload, rows_x, rows_y, depth_z):
    spectrum = jnp.stack([payload, jnp.zeros_like(payload)])
    fields_n = spectrum.shape[1]
    spectrum = transform(spectrum, 4, 1.0)
    spectrum = lax.all_to_all(spectrum, ("gy", "gz"), split_axis=4, concat_axis=3, tiled=True)
    groups_y = lax.axis_size(("gy", "gz"))
    span_z = spectrum.shape[4]
    blocks = spectrum.reshape((2, fields_n, rows_x + 1, groups_y, rows_y + 1, span_z))
    carried = jnp.roll(blocks[:, :, :, :, rows_y], 1, axis=3)
    first_row = blocks[:, :, :, :, 0] - carried
    blocks = jnp.concatenate([first_row[:, :, :, :, None], blocks[:, :, :, :, 1:rows_y]], axis=4)
    spectrum = blocks.reshape((2, fields_n, rows_x + 1, groups_y * rows_y, span_z))
    spectrum = transform(spectrum, 3, 1.0)
    spectrum = lax.all_to_all(spectrum, "gx", split_axis=3, concat_axis=2, tiled=True)
    groups_x = lax.axis_size("gx")
    span_y = spectrum.shape[3]
    blocks = spectrum.reshape((2, fields_n, groups_x, rows_x + 1, span_y, span_z))
    carried = jnp.roll(blocks[:, :, :, rows_x], 1, axis=2)
    first_row = blocks[:, :, :, 0] - carried
    blocks = jnp.concatenate([first_row[:, :, :, None], blocks[:, :, :, 1:rows_x]], axis=3)
    spectrum = blocks.reshape((2, fields_n, groups_x * rows_x, span_y, span_z))
    spectrum = transform(spectrum, 2, 1.0)
    length_x = groups_x * rows_x
    length_y = groups_y * rows_y
    freq_x = jnp.arange(length_x, dtype=jnp.float32)
    freq_y = (lax.axis_index("gx") * span_y + jnp.arange(span_y, dtype=jnp.int32)).astype(
        jnp.float32
    )
    freq_z = (lax.axis_index(("gy", "gz")) * span_z + jnp.arange(span_z, dtype=jnp.int32)).astype(
        jnp.float32
    )
    factor = laplace_factor(freq_x, freq_y, freq_z, length_x, length_y, depth_z) / float(
        length_x * length_y * depth_z
    )
    spectrum = spectrum * factor
    spectrum = transform(spectrum, 2, -1.0)
    blocks = spectrum.reshape((2, fields_n, groups_x, rows_x, span_y, span_z))
    following = jnp.roll(blocks[:, :, :, :1], -1, axis=2)
    spectrum = jnp.concatenate([blocks, following], axis=3).reshape(
        (2, fields_n, groups_x * (rows_x + 1), span_y, span_z)
    )
    spectrum = lax.all_to_all(spectrum, "gx", split_axis=2, concat_axis=3, tiled=True)
    spectrum = transform(spectrum, 3, -1.0)
    blocks = spectrum.reshape((2, fields_n, rows_x + 1, groups_y, rows_y, span_z))
    following = jnp.roll(blocks[:, :, :, :, :1], -1, axis=3)
    spectrum = jnp.concatenate([blocks, following], axis=4).reshape(
        (2, fields_n, rows_x + 1, groups_y * (rows_y + 1), span_z)
    )
    spectrum = lax.all_to_all(spectrum, ("gy", "gz"), split_axis=3, concat_axis=4, tiled=True)
    spectrum = transform(spectrum, 4, -1.0)
    return spectrum[0]


def cmul(a, b):
    return a[0] * b[0] - a[1] * b[1], a[0] * b[1] + a[1] * b[0]


def cadd(a, b):
    return a[0] + b[0], a[1] + b[1]


def conj(a):
    return a[0], -a[1]


def dot3(pairs):
    real = imag = None
    for a, b, flip_a, flip_b in pairs:
        rr, ii = a[0] * b[0], a[1] * b[1]
        ri, ir = a[0] * b[1], a[1] * b[0]
        r = rr - ii if flip_a == flip_b else rr + ii
        i = {(0, 0): lambda: ri + ir, (0, 1): lambda: ir - ri, (1, 0): lambda: ri - ir}[(flip_a, flip_b)]()
        real = r if real is None else real + r
        imag = i if imag is None else imag + i
    return real, imag


def mat_mul(a, b):
    return [[dot3([(a[r][m], b[m][c], 0, 0) for m in range(3)]) for c in range(3)] for r in range(3)]


def mat_mul_dag(a, b):
    return [[dot3([(a[r][m], b[c][m], 0, 1) for m in range(3)]) for c in range(3)] for r in range(3)]


def dag_mat_mul(a, b):
    return [[dot3([(a[m][r], b[m][c], 1, 0) for m in range(3)]) for c in range(3)] for r in range(3)]


def anti_parts(m):
    third = (m[0][0][1] + m[1][1][1] + m[2][2][1]) * (1.0 / 3.0)
    out = [m[0][0][1] - third, m[1][1][1] - third]
    for r, c in ((0, 1), (0, 2), (1, 2)):
        out.append(0.5 * (m[r][c][0] - m[c][r][0]))
        out.append(0.5 * (m[r][c][1] + m[c][r][1]))
    return out


def exp_parts(parts, scale):
    v = [0.5 * scale * p for p in parts]
    h0, h1 = v[0], v[1]
    h2 = -h0 - h1
    h01, h02, h12 = (v[3], -v[2]), (v[5], -v[4]), (v[7], -v[6])
    n01, n02, n12 = [h[0] * h[0] + h[1] * h[1] for h in (h01, h02, h12)]
    s0, s1, s2 = h0 * h0, h1 * h1, h2 * h2
    k00, k11, k22 = s0 + n01 + n02, s1 + n01 + n12, s2 + n02 + n12
    p02 = cmul(h01, h12)
    q = cmul(h02, conj(h12))
    w = cmul(conj(h01), h02)
    k01 = (q[0] - h2 * h01[0], q[1] - h2 * h01[1])
    k02 = (p02[0] - h1 * h02[0], p02[1] - h1 * h02[1])
    k12 = (w[0] - h0 * h12[0], w[1] - h0 * h12[1])
    t = 0.5 * (k00 + k11 + k22)
    d = h0 * h1 * h2 + 2.0 * (p02[0] * h02[0] + p02[1] * h02[1]) - h0 * n12 - h1 * n02 - h2 * n01
    t2 = t * t
    q0 = (1.0 - d * d * (1.0 / 720.0), d * (t * (1.0 / 120.0) - 1.0 / 6.0))
    q1 = (d * (1.0 / 24.0 - t * (1.0 / 360.0)), 1.0 - t * (1.0 / 6.0) + t2 * (1.0 / 120.0))
    q2 = (t * (1.0 / 24.0) - 0.5 - t2 * (1.0 / 720.0), d * (1.0 / 120.0))
    q00, q01, q02, q11, q12, q22 = cmul(q0, q0), cmul(q0, q1), cmul(q0, q2), cmul(q1, q1), cmul(q1, q2), cmul(q2, q2)
    e0 = [q00[n] + 2.0 * d * q12[n] for n in range(2)]
    e1 = [2.0 * (q01[n] + t * q12[n]) + d * q22[n] for n in range(2)]
    e2 = [2.0 * q02[n] + q11[n] + t * q22[n] for n in range(2)]
    out = [[None] * 3 for _ in range(3)]
    for r, (h, k) in enumerate(((h0, k00), (h1, k11), (h2, k22))):
        out[r][r] = (e0[0] + e1[0] * h + e2[0] * k, e0[1] + e1[1] * h + e2[1] * k)
    for r, c, h, k in ((0, 1, h01, k01), (0, 2, h02, k02), (1, 2, h12, k12)):
        out[r][c] = cadd(cmul(e1, h), cmul(e2, k))
        out[c][r] = cadd(cmul(e1, conj(h)), cmul(e2, conj(k)))
    return out


def mat_map(fn, m):
    return [[(fn(e[0]), fn(e[1])) for e in row] for row in m]


def load_mat(ref, base, x, row):
    return [
        [tuple(ref[base + 9 * part + 3 * r + c, x, row : row + 8, :] for part in range(2)) for c in range(3)]
        for r in range(3)
    ]


def forward_z(value):
    return pltpu.roll(value, value.shape[1] - 1, 1)


def backward_z(value):
    return pltpu.roll(value, 1, 1)


def staple_kernel(l_ref, hx_ref, hy_ref, gu_ref, lx_ref, ly_ref, rim_ref, ext):
    rows_x, rows_y = l_ref.shape[1], l_ref.shape[2]

    def fill(n, _):
        ext[n, 0:rows_x, 0:rows_y, :] = l_ref[n]
        return 0

    lax.fori_loop(0, 54, fill, 0)

    def fill_x(n, _):
        ext[18 + n, rows_x, 0:rows_y, :] = hx_ref[n]
        return 0

    lax.fori_loop(0, 36, fill_x, 0)
    for n in range(36):
        target = n if n < 18 else n + 18
        for x in range(rows_x):
            ext[target, x, rows_y : rows_y + 1, :] = hy_ref[x, n : n + 1, :]
    staple_planes(ext, gu_ref, lx_ref, ly_ref, rim_ref, lambda x: None)


def staple_planes(ext, gu_ref, lx_ref, ly_ref, rim_ref, arrive):
    rows_x, rows_y = gu_ref.shape[1], gu_ref.shape[2]

    def step(x, _):
        arrive(x)
        for row in (0, rows_y - 8):
            here = slice(row, row + 8)
            acc = [None] * 3

            def add(direction, parts, sign=1.0):
                if acc[direction] is None:
                    acc[direction] = parts if sign > 0 else [-p for p in parts]
                elif sign > 0:
                    acc[direction] = [p + q for p, q in zip(acc[direction], parts)]
                else:
                    acc[direction] = [p - q for p, q in zip(acc[direction], parts)]

            for i, j in ((0, 1), (0, 2), (1, 2)):
                ui, uj = load_mat(ext, 18 * i, x, row), load_mat(ext, 18 * j, x, row)
                if j == 1:
                    ui_j = load_mat(ext, 18 * i, x, row + 1)
                else:
                    ui_j = mat_map(forward_z, ui)
                if i == 0:
                    uj_i = load_mat(ext, 18 * j, x + 1, row)
                else:
                    uj_i = load_mat(ext, 18 * j, x, row + 1)
                b = mat_mul(ui, uj_i)
                a = mat_mul(uj, ui_j)
                plaquette = anti_parts(mat_mul_dag(a, b))
                add(i, plaquette)
                add(j, plaquette, -1.0)
                low_i = anti_parts(mat_mul_dag(dag_mat_mul(uj, b), ui_j))
                low_j = anti_parts(mat_mul_dag(dag_mat_mul(ui, a), uj_i))
                if j == 2:
                    add(i, [backward_z(p) for p in low_i])
                for parts, shift, slot in ((low_i, j, 0), (low_j, i, 0 if j == 1 else 8)):
                    for n, p in enumerate(parts):
                        if shift == 0:
                            lx_ref[slot + n, x + 1, here, :] = p
                        elif shift == 1:
                            ly_ref[slot + n, x, row + 1 : row + 9, :] = p
                            if row:
                                rim_ref[x, slot + n : slot + n + 1, :] = p[7:8, :]
            for direction in range(3):
                for n in range(8):
                    gu_ref[8 * direction + n, x, here, :] = acc[direction][n]
        return 0

    lax.fori_loop(0, rows_x, step, 0)


def smear_kernel(fast, l_ref, gu_ref, lx_ref, ly_ref, rx_ref, ry_ref, table_ref, v_ref, s_ref, a0, a1, dz, pack):
    smear_sites(fast, l_ref, gu_ref, lx_ref, ly_ref, rx_ref, ry_ref, table_ref, v_ref, s_ref, a0, a1, dz, pack, lambda x: None)


def smear_sites(fast, l_ref, gu_ref, lx_ref, ly_ref, rx_ref, ry_ref, table_ref, v_ref, s_ref, a0, a1, dz, pack, arrive):
    rows_x, rows_y = v_ref.shape[1], v_ref.shape[2]

    def step(n_step, _):
        x = rows_x - 1 - n_step
        arrive(x)
        for row in (0, rows_y - 8):
            here = slice(row, row + 8)
            top = lax.broadcasted_iota(jnp.int32, (8, 128), 0) == 0

            def low_x(n):
                if rx_ref is None:
                    return lx_ref[n, x, here, :]
                return jnp.where(x == 0, rx_ref[n, here, :], lx_ref[n, x, here, :])

            def low_y(n):
                value = ly_ref[n, x, here, :]
                if row == 0:
                    value = jnp.where(top, ry_ref[x, n : n + 1, :], value)
                return value

            for direction in range(3):
                parts = []
                for n in range(8):
                    p = gu_ref[8 * direction + n, x, here, :]
                    if direction == 0:
                        p = p + low_y(n)
                    elif direction == 1:
                        p = p + low_x(n)
                    else:
                        p = p + low_x(8 + n) + low_y(8 + n)
                    parts.append(p)
                smeared = mat_mul(exp_parts(parts, SMEAR_RHO), load_mat(l_ref, 18 * direction, x, row))
                for r in range(3):
                    for c in range(3):
                        for part in range(2):
                            v_ref[18 * direction + 9 * part + 3 * r + c, x, here, :] = smeared[r][c][part]
                for n, p in enumerate(anti_parts(smeared)):
                    if direction == 0:
                        a0[n, x, here, :] = p
                    elif direction == 1:
                        a1[n, x, row + 1 : row + 9, :] = p
                    else:
                        dz[n, x, here, :] = p - backward_z(p)
        return 0

    lax.fori_loop(0, rows_x, step, 0)

    def divergence(n, _):
        pack[n] = jnp.zeros(pack.shape[1:], jnp.float32)
        for x in range(rows_x):
            total = a0[n, x] + dz[n, x] + a1[n, x, 1 : rows_y + 1, :]
            if x:
                total = total - a0[n, x - 1]
            lanes = slice(128 * (x // 2), 128 * (x // 2) + 128)
            pack[n, x % 2, 0:rows_y, lanes] = total
            pack[n, x % 2, 1:rows_y, lanes] = pack[n, x % 2, 1:rows_y, lanes] - a1[n, x, 1:rows_y, :]
            pack[n, x % 2, rows_y : rows_y + 1, lanes] = a1[n, x, rows_y : rows_y + 1, :]
        pack[n, 1, 0:rows_y, 128:256] = a0[n, rows_x - 1]
        return 0

    lax.fori_loop(0, 8, divergence, 0)
    if fast:
        out = jnp.dot(
            pack[...].reshape(256, 256), table_ref[...], precision=HIGHEST, preferred_element_type=jnp.float32
        )
        for half in range(2):
            s_ref[:, half] = out[:, 128 * half : 128 * half + 128].reshape(8, 2, 16, 128)
    else:
        s_ref[...] = pack[...]


def solve_blocks(r_ref, ty_ref, tyi_ref, cf_ref, ci_ref, f_ref, o_ref, ready, done):
    half = lax.axis_index("gz")
    mine = lax.axis_index("gx")
    modes = [None] * 6
    for k in (0, 1, 3, 2):
        ready(k)
        gx = lax.rem(mine + 4 - k, 4)
        for xp in range(2):
            block = r_ref[pl.ds(4 * gx, 4), xp].reshape(64, 128)
            plane = jnp.dot(ty_ref[...], block, precision=HIGHEST, preferred_element_type=jnp.float32)
            turned = pltpu.roll(plane, 64, 1)
            for m in range(6):
                term = (
                    plane * cf_ref[2 * gx + xp, 2 * m : 2 * m + 1, :]
                    + turned * cf_ref[2 * gx + xp, 2 * m + 1 : 2 * m + 2, :]
                )
                modes[m] = term if modes[m] is None else modes[m] + term
    modes = [modes[m] * f_ref[half, m] for m in range(6)]
    turned = [pltpu.roll(p, 64, 1) for p in modes]
    for k in (2, 1, 3, 0):
        gx = lax.rem(mine + k, 4)
        for xp in range(2):
            total = None
            for m in range(6):
                term = (
                    modes[m] * ci_ref[2 * gx + xp, 2 * m : 2 * m + 1, :]
                    + turned[m] * ci_ref[2 * gx + xp, 2 * m + 1 : 2 * m + 2, :]
                )
                total = term if total is None else total + term
            out = jnp.dot(tyi_ref[...], total, precision=HIGHEST, preferred_element_type=jnp.float32)
            o_ref[pl.ds(4 * gx, 4), xp] = out.reshape(4, 16, 128)
        done(k)


def rotate_kernel(fast, q_ref, v_ref, table_ref, o_ref, acc, g, woven=False, finish=None):
    rows_x, rows_y = v_ref.shape[1], v_ref.shape[2]
    if fast:
        left = jnp.concatenate([q_ref[:, 0].reshape(256, 128), q_ref[:, 1].reshape(256, 128)], axis=1)
        out = jnp.dot(left, table_ref[...], precision=HIGHEST, preferred_element_type=jnp.float32)
        for part in range(2):
            acc[:, 2 * part : 2 * part + 2] = out[:, 128 * part : 128 * part + 128].reshape(8, 2, 16, 128)
        src = acc
    else:
        src = q_ref

    def exponent(x, _):
        for row in (0, 8):
            here = slice(row, row + 8)
            m = exp_parts([src[n, x, here, :] for n in range(8)], HALF_STEP)
            for r in range(3):
                for c in range(3):
                    for part in range(2):
                        g[9 * part + 3 * r + c, x, here, :] = m[r][c][part]
        return 0

    lax.fori_loop(0, rows_x + 1, exponent, 0)

    def step(x, _):
        for row in (0, rows_y - 8):
            here = slice(row, row + 8)
            centre = load_mat(g, 0, x, row)
            for direction in range(3):
                if direction == 0:
                    other = load_mat(g, 0, x + 1, row)
                elif direction == 1:
                    other = load_mat(g, 0, x, row + 1)
                else:
                    other = mat_map(forward_z, centre)
                out = mat_mul_dag(mat_mul(centre, load_mat(v_ref, 18 * direction, x, row)), other)
                for r in range(3):
                    for c in range(3):
                        for part in range(2):
                            if woven:
                                rows = pl.ds(2 * row + part, 8, stride=2)
                                o_ref[9 * direction + 3 * r + c, x, rows, :] = out[r][c][part]
                            else:
                                o_ref[18 * direction + 9 * part + 3 * r + c, x, here, :] = out[r][c][part]
        if finish is not None:
            finish(x)
        return 0

    lax.fori_loop(0, rows_x, step, 0)


def neighbour(axis_sizes, step_x, step_y):
    n_x, n_y, n_z = axis_sizes
    gx = lax.axis_index("gx")
    block = lax.axis_index("gy") * n_z + lax.axis_index("gz")
    if step_x:
        return {"gx": lax.rem(gx + n_x + step_x, n_x)}
    block = lax.rem(block + n_y * n_z + step_y, n_y * n_z)
    return {"gy": lax.div(block, n_z), "gz": lax.rem(block, n_z)}


def exchange_kernel(sizes, way, pick, sx_ref, sy_ref, rx_ref, ry_ref, send, recv):
    barrier = pltpu.get_barrier_semaphore()
    for device in (neighbour(sizes, -way, 0), neighbour(sizes, 0, -way)):
        pl.semaphore_signal(barrier, inc=1, device_id=device, device_id_type=MESH)
    pl.semaphore_wait(barrier, 2)
    first, count, x = pick
    copies = []
    for n, (src, dst, device) in enumerate(
        (
            (sx_ref.at[pl.ds(first, count), x], rx_ref, neighbour(sizes, way, 0)),
            (sy_ref, ry_ref, neighbour(sizes, 0, way)),
        )
    ):
        copies.append(
            pltpu.make_async_remote_copy(
                src_ref=src,
                dst_ref=dst,
                send_sem=send.at[n],
                recv_sem=recv.at[n],
                device_id=device,
                device_id_type=MESH,
            )
        )
        copies[-1].start()
    for copy in copies:
        copy.wait()


def exchange(sizes, way, pick, key, sx, sy):
    shapes = (
        jax.ShapeDtypeStruct((pick[1],) + sx.shape[2:], jnp.float32),
        jax.ShapeDtypeStruct(sy.shape, jnp.float32),
    )
    return pl.pallas_call(
        functools.partial(exchange_kernel, sizes, way, pick),
        out_shape=shapes,
        in_specs=[ANY, ANY],
        out_specs=(ANY, ANY),
        scratch_shapes=[pltpu.SemaphoreType.DMA((2,)), pltpu.SemaphoreType.DMA((2,))],
        compiler_params=pltpu.CompilerParams(collective_id=key, has_side_effects=True),
    )(sx, sy)


def real_basis(length):
    x = np.arange(length)
    freq = np.zeros(length, np.int64)
    rows = np.zeros((length, length))
    rows[0] = 1.0 / math.sqrt(length)
    for n in range(1, length):
        k = (n + 1) // 2
        freq[n] = k
        angle = 2.0 * math.pi * ((k * x) % length) / length
        if 2 * k == length:
            rows[n] = np.cos(angle) / math.sqrt(length)
        else:
            rows[n] = (np.cos(angle) if n % 2 else np.sin(angle)) * math.sqrt(2.0 / length)
    return rows, 4.0 * np.sin(math.pi * freq / length) ** 2


def tables():
    tz, pz = real_basis(128)
    ty, py = real_basis(48)
    tx, px = real_basis(12)
    wide = np.zeros((2, 128, 2, 2, 64))
    for p in range(2):
        wide[p, :, :, p, :] = tz.T.reshape(128, 2, 64)
    wide = wide.reshape(256, 256)
    fy = np.zeros((48, 4, 16))
    iy = np.zeros((4, 16, 48))
    for b in range(4):
        fy[:, b, :12] = ty[:, 12 * b : 12 * b + 12]
        fy[:, b, 12] = -ty[:, (12 * b + 12) % 48]
        for r in range(13):
            iy[b, r] = ty[:, (12 * b + r) % 48]
    cf = np.zeros((8, 6, 2, 2, 64))
    ci = np.zeros((8, 6, 2, 2, 64))
    factor = np.zeros((2, 6, 48, 2, 64))
    for m in range(6):
        for q in range(2):
            squared = px[m + 6 * q] + py[None, :, None] + pz.reshape(2, 1, 64)
            factor[:, m, :, q] = np.where(squared > 1e-9, 12.0 / np.where(squared > 1e-9, squared, 1.0), 0.0)
            for gx in range(4):
                for xp in range(2):
                    for turn in range(2):
                        x = xp + 2 * (q if turn == 0 else 1 - q)
                        kx = m + 6 * q
                        site = (3 * gx + x) % 12
                        cf[2 * gx + xp, m, turn, q] = -tx[kx, site] if x == 3 else tx[kx, site]
                        back = m + 6 * (q if turn == 0 else 1 - q)
                        ci[2 * gx + xp, m, turn, q] = tx[back, (3 * gx + xp + 2 * q) % 12]
    flat = lambda t, shape: jnp.asarray(t.reshape(shape), jnp.float32)
    return (
        flat(wide, (256, 256)),
        flat(wide.T.copy(), (256, 256)),
        flat(fy, (48, 64)),
        flat(iy, (64, 48)),
        flat(cf, (8, 12, 128)),
        flat(ci, (8, 12, 128)),
        flat(factor, (2, 6, 48, 128)),
    )


def local(kernel, shapes, scratch, *operands):
    single = isinstance(shapes[0], int)
    out = pl.pallas_call(
        kernel,
        out_shape=tuple(jax.ShapeDtypeStruct(s, jnp.float32) for s in ((shapes,) if single else shapes)),
        in_specs=[VMEM] * len(operands),
        out_specs=tuple(VMEM for _ in ((shapes,) if single else shapes)),
        scratch_shapes=[pltpu.VMEM(s, jnp.float32) for s in scratch],
        compiler_params=pltpu.CompilerParams(vmem_limit_bytes=40 << 20),
    )(*operands)
    return out[0] if single else out


def fused_kernel(sizes, *refs):
    l_ref, tables_hbm, o_ref = refs[0], refs[1:8], refs[8]
    tables_ref = refs[9:16]
    lv, hx, edge, hy, ext, gu, lx, ly, rim, ry, v, a0, a1, dz, pack, s, r, s2, q, acc, g, planes = refs[16:38]
    send, recv, near, out_sem = refs[38:]
    wide, wide_back, fy, iy, cf, ci, factor = tables_ref
    n_x, n_y, n_z = sizes
    total = n_x * n_y * n_z
    rows_x, rows_y = v.shape[1], v.shape[2]
    me = (lax.axis_index("gx") * n_y + lax.axis_index("gy")) * n_z + lax.axis_index("gz")

    def device(index):
        return {
            "gx": lax.div(index, n_y * n_z),
            "gy": lax.rem(lax.div(index, n_z), n_y),
            "gz": lax.rem(index, n_z),
        }

    pulls = [pltpu.make_async_copy(l_ref, lv, near.at[7])]
    pulls += [pltpu.make_async_copy(tables_hbm[n], tables_ref[n], near.at[n]) for n in range(7)]
    for pull in pulls:
        pull.start()
    r[...] = jnp.zeros(r.shape, jnp.float32)
    barrier = pltpu.get_barrier_semaphore()
    for offset in range(1, total):
        pl.semaphore_signal(
            barrier, inc=1, device_id=device(lax.rem(me + offset, total)), device_id_type=MESH
        )
    started = []

    def push(slot, src, dst, target):
        copy = pltpu.make_async_remote_copy(
            src_ref=src,
            dst_ref=dst,
            send_sem=send.at[slot],
            recv_sem=recv.at[slot],
            device_id=target,
            device_id_type=MESH,
        )
        copy.start()
        started.append(copy)
        return copy

    pl.semaphore_wait(barrier, total - 1)
    face = push(0, l_ref.at[pl.ds(9, 18), 0], hx, neighbour(sizes, -1, 0))
    pulls[0].wait()
    for d in range(3):

        def fill(n, _):
            for part in range(2):
                ext[18 * d + 9 * part + n, 0:rows_x, 0:rows_y, :] = lv[
                    9 * d + n, :, pl.ds(part, rows_y, stride=2), :
                ]
            return 0

        if d == 1:
            continue
        lax.fori_loop(0, 9, fill, 0)
    for n in range(36):
        source = n if n < 18 else n + 18
        for x in range(rows_x):
            edge[x, n : n + 1, :] = ext[source, x, 0:1, :]
    line = push(1, edge, hy, neighbour(sizes, 0, -1))

    def fill_middle(n, _):
        for part in range(2):
            ext[18 + 9 * part + n, 0:rows_x, 0:rows_y, :] = lv[9 + n, :, pl.ds(part, rows_y, stride=2), :]
        return 0

    lax.fori_loop(0, 9, fill_middle, 0)
    line.wait_recv()
    for n in range(36):
        target = n if n < 18 else n + 18
        for x in range(rows_x):
            ext[target, x, rows_y : rows_y + 1, :] = hy[x, n : n + 1, :]

    def face_arrives(x):
        @pl.when(x == rows_x - 1)
        def _():
            face.wait_recv()

            def fill_face(n, _):
                for d in range(2):
                    for part in range(2):
                        ext[18 * d + 18 + 9 * part + n, rows_x, 0:rows_y, :] = hx[
                            9 * d + n, pl.ds(part, rows_y, stride=2), :
                        ]
                return 0

            lax.fori_loop(0, 9, fill_face, 0)

    staple_planes(ext, gu, lx, ly, rim, face_arrives)
    low_line = push(3, rim, ry, neighbour(sizes, 0, 1))
    low_face = push(2, lx.at[:, rows_x], lx.at[:, 0], neighbour(sizes, 1, 0))
    pulls[1].wait()
    low_line.wait_recv()

    def low_face_arrives(x):
        @pl.when(x == 0)
        def _():
            low_face.wait_recv()

    smear_sites(True, ext, gu, lx, ly, None, ry, wide, v, s, a0, a1, dz, pack, low_face_arrives)
    used = rows_y + 1
    mine, spot = lax.div(me, 4), lax.rem(me, 4)
    there, back = {}, {}

    def partner(k, j):
        return 4 * lax.rem(mine + k, 4) + lax.rem(spot + j, 4)

    for k in (2, 1, 3, 0):
        for j in range(4):
            if k or j:
                peer = partner(k, j)
                there[k, j] = push(
                    3 + 4 * k + j,
                    s.at[lax.div(peer, 2), lax.rem(peer, 2), :, pl.ds(0, used)],
                    r.at[me, :, pl.ds(0, used)],
                    device(peer),
                )
    r[me, :, 0:used, :] = s[lax.div(me, 2), lax.rem(me, 2), :, 0:used, :]
    for pull in pulls[2:]:
        pull.wait()

    def ready(k):
        for j in range(4):
            if k or j:
                there[k, j].wait_recv()

    def done(k):
        for j in range(4):
            if k or j:
                peer = partner(k, j)
                back[k, j] = push(
                    18 + 4 * k + j,
                    s2.at[peer, :, pl.ds(0, used)],
                    q.at[lax.div(me, 2), lax.rem(me, 2), :, pl.ds(0, used)],
                    device(peer),
                )

    solve_blocks(r, fy, iy, cf, ci, factor, s2, ready, done)
    q[lax.div(me, 2), lax.rem(me, 2), :, 0:used, :] = s2[me, :, 0:used, :]
    for copy in back.values():
        copy.wait_recv()

    def store(x):
        return pltpu.make_async_copy(planes.at[:, x], o_ref.at[:, x], out_sem.at[x])

    rotate_kernel(True, q, v, wide_back, planes, acc, g, woven=True, finish=lambda x: store(x).start())
    for x in range(rows_x):
        store(x).wait()
    for copy in started:
        copy.wait_send()


def fused(sizes, gauge_links):
    rows_x, rows_y, depth = gauge_links.shape[4:]
    woven = jnp.transpose(gauge_links, (0, 2, 3, 4, 5, 1, 6)).reshape(27, rows_x, 2 * rows_y, depth)
    given = tables()
    shapes = [t.shape for t in given] + [
        woven.shape,
        (18, 2 * rows_y, depth),
        (rows_x, 36, depth),
        (rows_x, 36, depth),
        (54, rows_x + 1, 16, depth),
        (24, rows_x, rows_y, depth),
        (16, rows_x + 1, rows_y, depth),
        (16, rows_x, rows_y + 1, depth),
        (rows_x, 16, depth),
        (rows_x, 16, depth),
        (54, rows_x, rows_y, depth),
        (8, rows_x, rows_y, depth),
        (8, rows_x, rows_y + 1, depth),
        (8, rows_x, rows_y, depth),
        (8, 2, 16, 256),
        (8, 2, 2, 16, 128),
        (16, 2, 16, 128),
        (16, 2, 16, 128),
        (8, 2, 2, 16, 128),
        (8, 4, 16, 128),
        (18, rows_x + 1, 16, depth),
        woven.shape,
    ]
    out = pl.pallas_call(
        functools.partial(fused_kernel, sizes),
        out_shape=jax.ShapeDtypeStruct(woven.shape, jnp.float32),
        in_specs=[pl.BlockSpec(memory_space=pltpu.HBM)] * 8,
        out_specs=pl.BlockSpec(memory_space=pltpu.HBM),
        scratch_shapes=[pltpu.VMEM(shape, jnp.float32) for shape in shapes]
        + [
            pltpu.SemaphoreType.DMA((34,)),
            pltpu.SemaphoreType.DMA((34,)),
            pltpu.SemaphoreType.DMA((8,)),
            pltpu.SemaphoreType.DMA((rows_x,)),
        ],
        compiler_params=pltpu.CompilerParams(
            collective_id=5, has_side_effects=True, vmem_limit_bytes=(64 << 20) - (1 << 19)
        ),
    )(woven, *given)
    return jnp.transpose(out.reshape(3, 3, 3, rows_x, rows_y, 2, depth), (0, 5, 1, 2, 3, 4, 6))


def shards(sizes, gauge_links):
    if sizes == (4, 2, 2):
        return fused(sizes, gauge_links)
    rows_x, rows_y, depth = gauge_links.shape[4:]
    wide, wide_back = tables()[:2]
    links = gauge_links.reshape(54, rows_x, rows_y, depth)
    first = links[:, :, 0, :]
    edge = jnp.moveaxis(jnp.concatenate([first[:18], first[36:]], axis=0), 0, 1)
    hx, hy = exchange(sizes, -1, (18, 36, 0), 1, links, edge)
    gu, lx, ly, rim = local(
        staple_kernel,
        (
            (24, rows_x, rows_y, depth),
            (16, rows_x + 1, rows_y, depth),
            (16, rows_x, rows_y + 1, depth),
            (rows_x, 16, depth),
        ),
        [(54, rows_x + 1, 16, depth)],
        links,
        hx,
        hy,
    )
    rx, ry = exchange(sizes, 1, (0, 16, rows_x), 2, lx, rim)
    smeared, blocks = local(
        functools.partial(smear_kernel, False),
        ((54, rows_x, rows_y, depth), (8, 2, 16, 256)),
        [
            (8, rows_x, rows_y, depth),
            (8, rows_x, rows_y + 1, depth),
            (8, rows_x, rows_y, depth),
            (8, 2, 16, 256),
        ],
        links,
        gu,
        lx,
        ly,
        rx,
        ry,
        wide,
    )
    used = blocks[:, :, : rows_y + 1]
    payload = jnp.concatenate([used[..., :depth], used[..., depth:]], axis=1)
    accel = general_solve(payload, rows_x, rows_y, depth)
    accel = jnp.pad(accel, ((0, 0), (0, 0), (0, 16 - accel.shape[2]), (0, 0)))
    rotated = local(
        functools.partial(rotate_kernel, False),
        (54, rows_x, rows_y, depth),
        [(8, 4, 16, 128), (18, rows_x + 1, 16, depth)],
        accel,
        smeared,
        wide_back,
    )
    return rotated.reshape(gauge_links.shape)


def solution(mesh):
    sizes = (mesh.shape["gx"], mesh.shape["gy"], mesh.shape["gz"])
    return jax.shard_map(
        functools.partial(shards, sizes),
        mesh=mesh,
        in_specs=(P(None, None, None, None, ("slices", "gx"), ("gy", "gz"), None),),
        out_specs=P(None, None, None, None, ("slices", "gx"), ("gy", "gz"), None),
        check_vma=False,
    )
```

```python
import functools
import math

import jax
import jax.numpy as jnp
import numpy as np
from jax import lax
from jax.experimental import pallas as pl
from jax.experimental.pallas import tpu as pltpu
from jax.sharding import PartitionSpec as P

SMEAR_RHO = 0.1
HALF_STEP = -0.04
MESH = pl.DeviceIdType.MESH
HIGHEST = lax.Precision.HIGHEST
VMEM = pl.BlockSpec(memory_space=pltpu.VMEM)
ANY = pl.BlockSpec(memory_space=pl.ANY)


def laplace_factor(freq_x, freq_y, freq_z, count_x, count_y, count_z):
    sine_x = jnp.sin(math.pi * freq_x / count_x)
    sine_y = jnp.sin(math.pi * freq_y / count_y)
    sine_z = jnp.sin(math.pi * freq_z / count_z)
    squared = (
        4.0 * (sine_x * sine_x)[:, None, None]
        + 4.0 * (sine_y * sine_y)[None, :, None]
        + 4.0 * (sine_z * sine_z)[None, None, :]
    )
    positive = squared > 0.0
    return jnp.where(positive, 12.0 / jnp.where(positive, squared, 1.0), 0.0)


def dft_tables(length):
    positions = jnp.arange(length, dtype=jnp.int32)
    phases = positions[:, None] * positions[None, :] % length
    angles = phases.astype(jnp.float32) * (2.0 * math.pi / length)
    return (jnp.cos(angles), jnp.sin(angles))


def transform(spectrum, axis_pos, direction_sign):
    length = spectrum.shape[axis_pos]
    cosine_table, sine_table = dft_tables(length)
    highest = lax.Precision.HIGHEST
    real_part = jnp.moveaxis(spectrum[0], axis_pos - 1, -1)
    imag_part = jnp.moveaxis(spectrum[1], axis_pos - 1, -1)
    out_real = jnp.dot(real_part, cosine_table, precision=highest) + direction_sign * jnp.dot(
        imag_part, sine_table, precision=highest
    )
    out_imag = jnp.dot(imag_part, cosine_table, precision=highest) - direction_sign * jnp.dot(
        real_part, sine_table, precision=highest
    )
    return jnp.moveaxis(jnp.stack([out_real, out_imag]), -1, axis_pos)


def general_solve(payload, rows_x, rows_y, depth_z):
    spectrum = jnp.stack([payload, jnp.zeros_like(payload)])
    fields_n = spectrum.shape[1]
    spectrum = transform(spectrum, 4, 1.0)
    spectrum = lax.all_to_all(spectrum, ("gy", "gz"), split_axis=4, concat_axis=3, tiled=True)
    groups_y = lax.axis_size(("gy", "gz"))
    span_z = spectrum.shape[4]
    blocks = spectrum.reshape((2, fields_n, rows_x + 1, groups_y, rows_y + 1, span_z))
    carried = jnp.roll(blocks[:, :, :, :, rows_y], 1, axis=3)
    first_row = blocks[:, :, :, :, 0] - carried
    blocks = jnp.concatenate([first_row[:, :, :, :, None], blocks[:, :, :, :, 1:rows_y]], axis=4)
    spectrum = blocks.reshape((2, fields_n, rows_x + 1, groups_y * rows_y, span_z))
    spectrum = transform(spectrum, 3, 1.0)
    spectrum = lax.all_to_all(spectrum, "gx", split_axis=3, concat_axis=2, tiled=True)
    groups_x = lax.axis_size("gx")
    span_y = spectrum.shape[3]
    blocks = spectrum.reshape((2, fields_n, groups_x, rows_x + 1, span_y, span_z))
    carried = jnp.roll(blocks[:, :, :, rows_x], 1, axis=2)
    first_row = blocks[:, :, :, 0] - carried
    blocks = jnp.concatenate([first_row[:, :, :, None], blocks[:, :, :, 1:rows_x]], axis=3)
    spectrum = blocks.reshape((2, fields_n, groups_x * rows_x, span_y, span_z))
    spectrum = transform(spectrum, 2, 1.0)
    length_x = groups_x * rows_x
    length_y = groups_y * rows_y
    freq_x = jnp.arange(length_x, dtype=jnp.float32)
    freq_y = (lax.axis_index("gx") * span_y + jnp.arange(span_y, dtype=jnp.int32)).astype(
        jnp.float32
    )
    freq_z = (lax.axis_index(("gy", "gz")) * span_z + jnp.arange(span_z, dtype=jnp.int32)).astype(
        jnp.float32
    )
    factor = laplace_factor(freq_x, freq_y, freq_z, length_x, length_y, depth_z) / float(
        length_x * length_y * depth_z
    )
    spectrum = spectrum * factor
    spectrum = transform(spectrum, 2, -1.0)
    blocks = spectrum.reshape((2, fields_n, groups_x, rows_x, span_y, span_z))
    following = jnp.roll(blocks[:, :, :, :1], -1, axis=2)
    spectrum = jnp.concatenate([blocks, following], axis=3).reshape(
        (2, fields_n, groups_x * (rows_x + 1), span_y, span_z)
    )
    spectrum = lax.all_to_all(spectrum, "gx", split_axis=2, concat_axis=3, tiled=True)
    spectrum = transform(spectrum, 3, -1.0)
    blocks = spectrum.reshape((2, fields_n, rows_x + 1, groups_y, rows_y, span_z))
    following = jnp.roll(blocks[:, :, :, :, :1], -1, axis=3)
    spectrum = jnp.concatenate([blocks, following], axis=4).reshape(
        (2, fields_n, rows_x + 1, groups_y * (rows_y + 1), span_z)
    )
    spectrum = lax.all_to_all(spectrum, ("gy", "gz"), split_axis=3, concat_axis=4, tiled=True)
    spectrum = transform(spectrum, 4, -1.0)
    return spectrum[0]


def cmul(a, b):
    return a[0] * b[0] - a[1] * b[1], a[0] * b[1] + a[1] * b[0]


def cadd(a, b):
    return a[0] + b[0], a[1] + b[1]


def conj(a):
    return a[0], -a[1]


def dot3(pairs):
    real = imag = None
    for a, b, flip_a, flip_b in pairs:
        rr, ii = a[0] * b[0], a[1] * b[1]
        ri, ir = a[0] * b[1], a[1] * b[0]
        r = rr - ii if flip_a == flip_b else rr + ii
        i = {(0, 0): lambda: ri + ir, (0, 1): lambda: ir - ri, (1, 0): lambda: ri - ir}[(flip_a, flip_b)]()
        real = r if real is None else real + r
        imag = i if imag is None else imag + i
    return real, imag


def mat_mul(a, b):
    return [[dot3([(a[r][m], b[m][c], 0, 0) for m in range(3)]) for c in range(3)] for r in range(3)]


def mat_mul_dag(a, b):
    return [[dot3([(a[r][m], b[c][m], 0, 1) for m in range(3)]) for c in range(3)] for r in range(3)]


def dag_mat_mul(a, b):
    return [[dot3([(a[m][r], b[m][c], 1, 0) for m in range(3)]) for c in range(3)] for r in range(3)]


def anti_parts(m):
    third = (m[0][0][1] + m[1][1][1] + m[2][2][1]) * (1.0 / 3.0)
    out = [m[0][0][1] - third, m[1][1][1] - third]
    for r, c in ((0, 1), (0, 2), (1, 2)):
        out.append(0.5 * (m[r][c][0] - m[c][r][0]))
        out.append(0.5 * (m[r][c][1] + m[c][r][1]))
    return out


def exp_parts(parts, scale):
    v = [0.5 * scale * p for p in parts]
    h0, h1 = v[0], v[1]
    h2 = -h0 - h1
    h01, h02, h12 = (v[3], -v[2]), (v[5], -v[4]), (v[7], -v[6])
    n01, n02, n12 = [h[0] * h[0] + h[1] * h[1] for h in (h01, h02, h12)]
    s0, s1, s2 = h0 * h0, h1 * h1, h2 * h2
    k00, k11, k22 = s0 + n01 + n02, s1 + n01 + n12, s2 + n02 + n12
    p02 = cmul(h01, h12)
    q = cmul(h02, conj(h12))
    w = cmul(conj(h01), h02)
    k01 = (q[0] - h2 * h01[0], q[1] - h2 * h01[1])
    k02 = (p02[0] - h1 * h02[0], p02[1] - h1 * h02[1])
    k12 = (w[0] - h0 * h12[0], w[1] - h0 * h12[1])
    t = 0.5 * (k00 + k11 + k22)
    d = h0 * h1 * h2 + 2.0 * (p02[0] * h02[0] + p02[1] * h02[1]) - h0 * n12 - h1 * n02 - h2 * n01
    t2 = t * t
    q0 = (1.0 - d * d * (1.0 / 720.0), d * (t * (1.0 / 120.0) - 1.0 / 6.0))
    q1 = (d * (1.0 / 24.0 - t * (1.0 / 360.0)), 1.0 - t * (1.0 / 6.0) + t2 * (1.0 / 120.0))
    q2 = (t * (1.0 / 24.0) - 0.5 - t2 * (1.0 / 720.0), d * (1.0 / 120.0))
    q00, q01, q02, q11, q12, q22 = cmul(q0, q0), cmul(q0, q1), cmul(q0, q2), cmul(q1, q1), cmul(q1, q2), cmul(q2, q2)
    e0 = [q00[n] + 2.0 * d * q12[n] for n in range(2)]
    e1 = [2.0 * (q01[n] + t * q12[n]) + d * q22[n] for n in range(2)]
    e2 = [2.0 * q02[n] + q11[n] + t * q22[n] for n in range(2)]
    out = [[None] * 3 for _ in range(3)]
    for r, (h, k) in enumerate(((h0, k00), (h1, k11), (h2, k22))):
        out[r][r] = (e0[0] + e1[0] * h + e2[0] * k, e0[1] + e1[1] * h + e2[1] * k)
    for r, c, h, k in ((0, 1, h01, k01), (0, 2, h02, k02), (1, 2, h12, k12)):
        out[r][c] = cadd(cmul(e1, h), cmul(e2, k))
        out[c][r] = cadd(cmul(e1, conj(h)), cmul(e2, conj(k)))
    return out


def mat_map(fn, m):
    return [[(fn(e[0]), fn(e[1])) for e in row] for row in m]


def load_mat(ref, base, x, row):
    return [
        [tuple(ref[base + 9 * part + 3 * r + c, x, row : row + 8, :] for part in range(2)) for c in range(3)]
        for r in range(3)
    ]


def forward_z(value):
    return pltpu.roll(value, value.shape[1] - 1, 1)


def backward_z(value):
    return pltpu.roll(value, 1, 1)


def staple_kernel(l_ref, hx_ref, hy_ref, gu_ref, lx_ref, ly_ref, rim_ref, ext):
    rows_x, rows_y = l_ref.shape[1], l_ref.shape[2]

    def fill(n, _):
        ext[n, 0:rows_x, 0:rows_y, :] = l_ref[n]
        return 0

    lax.fori_loop(0, 54, fill, 0)

    def fill_x(n, _):
        ext[18 + n, rows_x, 0:rows_y, :] = hx_ref[n]
        return 0

    lax.fori_loop(0, 36, fill_x, 0)
    for n in range(36):
        target = n if n < 18 else n + 18
        for x in range(rows_x):
            ext[target, x, rows_y : rows_y + 1, :] = hy_ref[x, n : n + 1, :]
    staple_planes(ext, gu_ref, lx_ref, ly_ref, rim_ref, lambda x: None)


def staple_planes(ext, gu_ref, lx_ref, ly_ref, rim_ref, arrive):
    rows_x, rows_y = gu_ref.shape[1], gu_ref.shape[2]

    def step(x, _):
        arrive(x)
        for row in (0, rows_y - 8):
            here = slice(row, row + 8)
            acc = [None] * 3

            def add(direction, parts, sign=1.0):
                if acc[direction] is None:
                    acc[direction] = parts if sign > 0 else [-p for p in parts]
                elif sign > 0:
                    acc[direction] = [p + q for p, q in zip(acc[direction], parts)]
                else:
                    acc[direction] = [p - q for p, q in zip(acc[direction], parts)]

            for i, j in ((0, 1), (0, 2), (1, 2)):
                ui, uj = load_mat(ext, 18 * i, x, row), load_mat(ext, 18 * j, x, row)
                if j == 1:
                    ui_j = load_mat(ext, 18 * i, x, row + 1)
                else:
                    ui_j = mat_map(forward_z, ui)
                if i == 0:
                    uj_i = load_mat(ext, 18 * j, x + 1, row)
                else:
                    uj_i = load_mat(ext, 18 * j, x, row + 1)
                b = mat_mul(ui, uj_i)
                a = mat_mul(uj, ui_j)
                plaquette = anti_parts(mat_mul_dag(a, b))
                add(i, plaquette)
                add(j, plaquette, -1.0)
                low_i = anti_parts(mat_mul_dag(dag_mat_mul(uj, b), ui_j))
                low_j = anti_parts(mat_mul_dag(dag_mat_mul(ui, a), uj_i))
                if j == 2:
                    add(i, [backward_z(p) for p in low_i])
                for parts, shift, slot in ((low_i, j, 0), (low_j, i, 0 if j == 1 else 8)):
                    for n, p in enumerate(parts):
                        if shift == 0:
                            lx_ref[slot + n, x + 1, here, :] = p
                        elif shift == 1:
                            ly_ref[slot + n, x, row + 1 : row + 9, :] = p
                            if row:
                                rim_ref[x, slot + n : slot + n + 1, :] = p[7:8, :]
            for direction in range(3):
                for n in range(8):
                    gu_ref[8 * direction + n, x, here, :] = acc[direction][n]
        return 0

    lax.fori_loop(0, rows_x, step, 0)


def smear_kernel(fast, l_ref, gu_ref, lx_ref, ly_ref, rx_ref, ry_ref, table_ref, v_ref, s_ref, a0, a1, dz, pack):
    smear_sites(fast, l_ref, gu_ref, lx_ref, ly_ref, rx_ref, ry_ref, table_ref, v_ref, s_ref, a0, a1, dz, pack, lambda x: None)


def smear_sites(fast, l_ref, gu_ref, lx_ref, ly_ref, rx_ref, ry_ref, table_ref, v_ref, s_ref, a0, a1, dz, pack, arrive):
    rows_x, rows_y = v_ref.shape[1], v_ref.shape[2]

    def step(n_step, _):
        x = rows_x - 1 - n_step
        arrive(x)
        for row in (0, rows_y - 8):
            here = slice(row, row + 8)
            top = lax.broadcasted_iota(jnp.int32, (8, 128), 0) == 0

            def low_x(n):
                if rx_ref is None:
                    return lx_ref[n, x, here, :]
                return jnp.where(x == 0, rx_ref[n, here, :], lx_ref[n, x, here, :])

            def low_y(n):
                value = ly_ref[n, x, here, :]
                if row == 0:
                    value = jnp.where(top, ry_ref[x, n : n + 1, :], value)
                return value

            for direction in range(3):
                parts = []
                for n in range(8):
                    p = gu_ref[8 * direction + n, x, here, :]
                    if direction == 0:
                        p = p + low_y(n)
                    elif direction == 1:
                        p = p + low_x(n)
                    else:
                        p = p + low_x(8 + n) + low_y(8 + n)
                    parts.append(p)
                smeared = mat_mul(exp_parts(parts, SMEAR_RHO), load_mat(l_ref, 18 * direction, x, row))
                for r in range(3):
                    for c in range(3):
                        for part in range(2):
                            v_ref[18 * direction + 9 * part + 3 * r + c, x, here, :] = smeared[r][c][part]
                for n, p in enumerate(anti_parts(smeared)):
                    if direction == 0:
                        a0[n, x, here, :] = p
                    elif direction == 1:
                        a1[n, x, row + 1 : row + 9, :] = p
                    else:
                        dz[n, x, here, :] = p - backward_z(p)
        return 0

    lax.fori_loop(0, rows_x, step, 0)

    def divergence(n, _):
        pack[n] = jnp.zeros(pack.shape[1:], jnp.float32)
        for x in range(rows_x):
            total = a0[n, x] + dz[n, x] + a1[n, x, 1 : rows_y + 1, :]
            if x:
                total = total - a0[n, x - 1]
            lanes = slice(128 * (x // 2), 128 * (x // 2) + 128)
            pack[n, x % 2, 0:rows_y, lanes] = total
            pack[n, x % 2, 1:rows_y, lanes] = pack[n, x % 2, 1:rows_y, lanes] - a1[n, x, 1:rows_y, :]
            pack[n, x % 2, rows_y : rows_y + 1, lanes] = a1[n, x, rows_y : rows_y + 1, :]
        pack[n, 1, 0:rows_y, 128:256] = a0[n, rows_x - 1]
        return 0

    lax.fori_loop(0, 8, divergence, 0)
    if fast:
        out = jnp.dot(
            pack[...].reshape(256, 256), table_ref[...], precision=HIGHEST, preferred_element_type=jnp.float32
        )
        for half in range(2):
            s_ref[:, half] = out[:, 128 * half : 128 * half + 128].reshape(8, 2, 16, 128)
    else:
        s_ref[...] = pack[...]


def solve_blocks(r_ref, ty_ref, tyi_ref, cf_ref, ci_ref, f_ref, o_ref, ready, done):
    half = lax.axis_index("gz")
    mine = lax.axis_index("gx")
    modes = [None] * 6
    for k in (0, 1, 3, 2):
        ready(k)
        gx = lax.rem(mine + 4 - k, 4)
        for xp in range(2):
            block = r_ref[pl.ds(4 * gx, 4), xp].reshape(64, 128)
            plane = jnp.dot(ty_ref[...], block, precision=HIGHEST, preferred_element_type=jnp.float32)
            turned = pltpu.roll(plane, 64, 1)
            for m in range(6):
                term = (
                    plane * cf_ref[2 * gx + xp, 2 * m : 2 * m + 1, :]
                    + turned * cf_ref[2 * gx + xp, 2 * m + 1 : 2 * m + 2, :]
                )
                modes[m] = term if modes[m] is None else modes[m] + term
    modes = [modes[m] * f_ref[half, m] for m in range(6)]
    turned = [pltpu.roll(p, 64, 1) for p in modes]
    for k in (2, 1, 3, 0):
        gx = lax.rem(mine + k, 4)
        for xp in range(2):
            total = None
            for m in range(6):
                term = (
                    modes[m] * ci_ref[2 * gx + xp, 2 * m : 2 * m + 1, :]
                    + turned[m] * ci_ref[2 * gx + xp, 2 * m + 1 : 2 * m + 2, :]
                )
                total = term if total is None else total + term
            out = jnp.dot(tyi_ref[...], total, precision=HIGHEST, preferred_element_type=jnp.float32)
            o_ref[pl.ds(4 * gx, 4), xp] = out.reshape(4, 16, 128)
        done(k)


def rotate_kernel(fast, q_ref, v_ref, table_ref, o_ref, acc, g, woven=False, finish=None):
    rows_x, rows_y = v_ref.shape[1], v_ref.shape[2]
    if fast:
        left = jnp.concatenate([q_ref[:, 0].reshape(256, 128), q_ref[:, 1].reshape(256, 128)], axis=1)
        out = jnp.dot(left, table_ref[...], precision=HIGHEST, preferred_element_type=jnp.float32)
        for part in range(2):
            acc[:, 2 * part : 2 * part + 2] = out[:, 128 * part : 128 * part + 128].reshape(8, 2, 16, 128)
        src = acc
    else:
        src = q_ref

    def exponent(x, _):
        for row in (0, 8):
            here = slice(row, row + 8)
            m = exp_parts([src[n, x, here, :] for n in range(8)], HALF_STEP)
            for r in range(3):
                for c in range(3):
                    for part in range(2):
                        g[9 * part + 3 * r + c, x, here, :] = m[r][c][part]
        return 0

    lax.fori_loop(0, rows_x + 1, exponent, 0)

    def step(x, _):
        for row in (0, rows_y - 8):
            here = slice(row, row + 8)
            centre = load_mat(g, 0, x, row)
            for direction in range(3):
                if direction == 0:
                    other = load_mat(g, 0, x + 1, row)
                elif direction == 1:
                    other = load_mat(g, 0, x, row + 1)
                else:
                    other = mat_map(forward_z, centre)
                out = mat_mul_dag(mat_mul(centre, load_mat(v_ref, 18 * direction, x, row)), other)
                for r in range(3):
                    for c in range(3):
                        for part in range(2):
                            if woven:
                                rows = pl.ds(2 * row + part, 8, stride=2)
                                o_ref[9 * direction + 3 * r + c, x, rows, :] = out[r][c][part]
                            else:
                                o_ref[18 * direction + 9 * part + 3 * r + c, x, here, :] = out[r][c][part]
        if finish is not None:
            finish(x)
        return 0

    lax.fori_loop(0, rows_x, step, 0)


def neighbour(axis_sizes, step_x, step_y):
    n_x, n_y, n_z = axis_sizes
    gx = lax.axis_index("gx")
    block = lax.axis_index("gy") * n_z + lax.axis_index("gz")
    if step_x:
        return {"gx": lax.rem(gx + n_x + step_x, n_x)}
    block = lax.rem(block + n_y * n_z + step_y, n_y * n_z)
    return {"gy": lax.div(block, n_z), "gz": lax.rem(block, n_z)}


def exchange_kernel(sizes, way, pick, sx_ref, sy_ref, rx_ref, ry_ref, send, recv):
    barrier = pltpu.get_barrier_semaphore()
    for device in (neighbour(sizes, -way, 0), neighbour(sizes, 0, -way)):
        pl.semaphore_signal(barrier, inc=1, device_id=device, device_id_type=MESH)
    pl.semaphore_wait(barrier, 2)
    first, count, x = pick
    copies = []
    for n, (src, dst, device) in enumerate(
        (
            (sx_ref.at[pl.ds(first, count), x], rx_ref, neighbour(sizes, way, 0)),
            (sy_ref, ry_ref, neighbour(sizes, 0, way)),
        )
    ):
        copies.append(
            pltpu.make_async_remote_copy(
                src_ref=src,
                dst_ref=dst,
                send_sem=send.at[n],
                recv_sem=recv.at[n],
                device_id=device,
                device_id_type=MESH,
            )
        )
        copies[-1].start()
    for copy in copies:
        copy.wait()


def exchange(sizes, way, pick, key, sx, sy):
    shapes = (
        jax.ShapeDtypeStruct((pick[1],) + sx.shape[2:], jnp.float32),
        jax.ShapeDtypeStruct(sy.shape, jnp.float32),
    )
    return pl.pallas_call(
        functools.partial(exchange_kernel, sizes, way, pick),
        out_shape=shapes,
        in_specs=[ANY, ANY],
        out_specs=(ANY, ANY),
        scratch_shapes=[pltpu.SemaphoreType.DMA((2,)), pltpu.SemaphoreType.DMA((2,))],
        compiler_params=pltpu.CompilerParams(collective_id=key, has_side_effects=True),
    )(sx, sy)


def real_basis(length):
    x = np.arange(length)
    freq = np.zeros(length, np.int64)
    rows = np.zeros((length, length))
    rows[0] = 1.0 / math.sqrt(length)
    for n in range(1, length):
        k = (n + 1) // 2
        freq[n] = k
        angle = 2.0 * math.pi * ((k * x) % length) / length
        if 2 * k == length:
            rows[n] = np.cos(angle) / math.sqrt(length)
        else:
            rows[n] = (np.cos(angle) if n % 2 else np.sin(angle)) * math.sqrt(2.0 / length)
    return rows, 4.0 * np.sin(math.pi * freq / length) ** 2


def tables():
    tz, pz = real_basis(128)
    ty, py = real_basis(48)
    tx, px = real_basis(12)
    wide = np.zeros((2, 128, 2, 2, 64))
    for p in range(2):
        wide[p, :, :, p, :] = tz.T.reshape(128, 2, 64)
    wide = wide.reshape(256, 256)
    fy = np.zeros((48, 4, 16))
    iy = np.zeros((4, 16, 48))
    for b in range(4):
        fy[:, b, :12] = ty[:, 12 * b : 12 * b + 12]
        fy[:, b, 12] = -ty[:, (12 * b + 12) % 48]
        for r in range(13):
            iy[b, r] = ty[:, (12 * b + r) % 48]
    cf = np.zeros((8, 6, 2, 2, 64))
    ci = np.zeros((8, 6, 2, 2, 64))
    factor = np.zeros((2, 6, 48, 2, 64))
    for m in range(6):
        for q in range(2):
            squared = px[m + 6 * q] + py[None, :, None] + pz.reshape(2, 1, 64)
            factor[:, m, :, q] = np.where(squared > 1e-9, 12.0 / np.where(squared > 1e-9, squared, 1.0), 0.0)
            for gx in range(4):
                for xp in range(2):
                    for turn in range(2):
                        x = xp + 2 * (q if turn == 0 else 1 - q)
                        kx = m + 6 * q
                        site = (3 * gx + x) % 12
                        cf[2 * gx + xp, m, turn, q] = -tx[kx, site] if x == 3 else tx[kx, site]
                        back = m + 6 * (q if turn == 0 else 1 - q)
                        ci[2 * gx + xp, m, turn, q] = tx[back, (3 * gx + xp + 2 * q) % 12]
    flat = lambda t, shape: jnp.asarray(t.reshape(shape), jnp.float32)
    return (
        flat(wide, (256, 256)),
        flat(wide.T.copy(), (256, 256)),
        flat(fy, (48, 64)),
        flat(iy, (64, 48)),
        flat(cf, (8, 12, 128)),
        flat(ci, (8, 12, 128)),
        flat(factor, (2, 6, 48, 128)),
    )


def local(kernel, shapes, scratch, *operands):
    single = isinstance(shapes[0], int)
    out = pl.pallas_call(
        kernel,
        out_shape=tuple(jax.ShapeDtypeStruct(s, jnp.float32) for s in ((shapes,) if single else shapes)),
        in_specs=[VMEM] * len(operands),
        out_specs=tuple(VMEM for _ in ((shapes,) if single else shapes)),
        scratch_shapes=[pltpu.VMEM(s, jnp.float32) for s in scratch],
        compiler_params=pltpu.CompilerParams(vmem_limit_bytes=40 << 20),
    )(*operands)
    return out[0] if single else out


def fused_kernel(sizes, *refs):
    l_ref, tables_hbm, o_ref = refs[0], refs[1:8], refs[8]
    tables_ref = refs[9:16]
    lv, hx, edge, hy, ext, gu, lx, ly, rim, ry, v, a0, a1, dz, pack, s, r, s2, q, acc, g, planes = refs[16:38]
    send, recv, near, out_sem = refs[38:]
    wide, wide_back, fy, iy, cf, ci, factor = tables_ref
    n_x, n_y, n_z = sizes
    total = n_x * n_y * n_z
    rows_x, rows_y = v.shape[1], v.shape[2]
    me = (lax.axis_index("gx") * n_y + lax.axis_index("gy")) * n_z + lax.axis_index("gz")

    def device(index):
        return {
            "gx": lax.div(index, n_y * n_z),
            "gy": lax.rem(lax.div(index, n_z), n_y),
            "gz": lax.rem(index, n_z),
        }

    pulls = [pltpu.make_async_copy(l_ref, lv, near.at[7])]
    pulls += [pltpu.make_async_copy(tables_hbm[n], tables_ref[n], near.at[n]) for n in range(7)]
    for pull in pulls:
        pull.start()
    r[...] = jnp.zeros(r.shape, jnp.float32)
    barrier = pltpu.get_barrier_semaphore()
    for offset in range(1, total):
        pl.semaphore_signal(
            barrier, inc=1, device_id=device(lax.rem(me + offset, total)), device_id_type=MESH
        )
    started = []

    def push(slot, src, dst, target):
        copy = pltpu.make_async_remote_copy(
            src_ref=src,
            dst_ref=dst,
            send_sem=send.at[slot],
            recv_sem=recv.at[slot],
            device_id=target,
            device_id_type=MESH,
        )
        copy.start()
        started.append(copy)
        return copy

    pl.semaphore_wait(barrier, total - 1)
    faces = [
        push(slot, l_ref.at[pl.ds(9 + first, 9), 0], hx.at[pl.ds(first, 9)], neighbour(sizes, -1, 0))
        for slot, first in ((0, 0), (34, 9))
    ]
    pulls[0].wait()
    for d in range(3):

        def fill(n, _):
            for part in range(2):
                ext[18 * d + 9 * part + n, 0:rows_x, 0:rows_y, :] = lv[
                    9 * d + n, :, pl.ds(part, rows_y, stride=2), :
                ]
            return 0

        if d == 1:
            continue
        lax.fori_loop(0, 9, fill, 0)
    for n in range(36):
        source = n if n < 18 else n + 18
        for x in range(rows_x):
            edge[x, n : n + 1, :] = ext[source, x, 0:1, :]
    line = push(1, edge, hy, neighbour(sizes, 0, -1))

    def fill_middle(n, _):
        for part in range(2):
            ext[18 + 9 * part + n, 0:rows_x, 0:rows_y, :] = lv[9 + n, :, pl.ds(part, rows_y, stride=2), :]
        return 0

    lax.fori_loop(0, 9, fill_middle, 0)
    line.wait_recv()
    for n in range(36):
        target = n if n < 18 else n + 18
        for x in range(rows_x):
            ext[target, x, rows_y : rows_y + 1, :] = hy[x, n : n + 1, :]

    def face_arrives(x):
        @pl.when(x == rows_x - 1)
        def _():
            for face in faces:
                face.wait_recv()

            def fill_face(n, _):
                for d in range(2):
                    for part in range(2):
                        ext[18 * d + 18 + 9 * part + n, rows_x, 0:rows_y, :] = hx[
                            9 * d + n, pl.ds(part, rows_y, stride=2), :
                        ]
                return 0

            lax.fori_loop(0, 9, fill_face, 0)

    staple_planes(ext, gu, lx, ly, rim, face_arrives)
    low_line = push(3, rim, ry, neighbour(sizes, 0, 1))
    low_face = push(2, lx.at[:, rows_x], lx.at[:, 0], neighbour(sizes, 1, 0))
    pulls[1].wait()
    low_line.wait_recv()

    def low_face_arrives(x):
        @pl.when(x == 0)
        def _():
            low_face.wait_recv()

    smear_sites(True, ext, gu, lx, ly, None, ry, wide, v, s, a0, a1, dz, pack, low_face_arrives)
    used = rows_y + 1
    mine, spot = lax.div(me, 4), lax.rem(me, 4)
    there, back = {}, {}

    def partner(k, j):
        return 4 * lax.rem(mine + k, 4) + lax.rem(spot + j, 4)

    for k in (2, 1, 3, 0):
        for j in range(4):
            if k or j:
                peer = partner(k, j)
                there[k, j] = push(
                    3 + 4 * k + j,
                    s.at[lax.div(peer, 2), lax.rem(peer, 2), :, pl.ds(0, used)],
                    r.at[me, :, pl.ds(0, used)],
                    device(peer),
                )
    r[me, :, 0:used, :] = s[lax.div(me, 2), lax.rem(me, 2), :, 0:used, :]
    for pull in pulls[2:]:
        pull.wait()

    def ready(k):
        for j in range(4):
            if k or j:
                there[k, j].wait_recv()

    def done(k):
        for j in range(4):
            if k or j:
                peer = partner(k, j)
                back[k, j] = push(
                    18 + 4 * k + j,
                    s2.at[peer, :, pl.ds(0, used)],
                    q.at[lax.div(me, 2), lax.rem(me, 2), :, pl.ds(0, used)],
                    device(peer),
                )

    solve_blocks(r, fy, iy, cf, ci, factor, s2, ready, done)
    q[lax.div(me, 2), lax.rem(me, 2), :, 0:used, :] = s2[me, :, 0:used, :]
    for copy in back.values():
        copy.wait_recv()

    def store(x):
        return pltpu.make_async_copy(planes.at[:, x], o_ref.at[:, x], out_sem.at[x])

    rotate_kernel(True, q, v, wide_back, planes, acc, g, woven=True, finish=lambda x: store(x).start())
    for x in range(rows_x):
        store(x).wait()
    for copy in started:
        copy.wait_send()


def fused(sizes, gauge_links):
    rows_x, rows_y, depth = gauge_links.shape[4:]
    woven = jnp.transpose(gauge_links, (0, 2, 3, 4, 5, 1, 6)).reshape(27, rows_x, 2 * rows_y, depth)
    given = tables()
    shapes = [t.shape for t in given] + [
        woven.shape,
        (18, 2 * rows_y, depth),
        (rows_x, 36, depth),
        (rows_x, 36, depth),
        (54, rows_x + 1, 16, depth),
        (24, rows_x, rows_y, depth),
        (16, rows_x + 1, rows_y, depth),
        (16, rows_x, rows_y + 1, depth),
        (rows_x, 16, depth),
        (rows_x, 16, depth),
        (54, rows_x, rows_y, depth),
        (8, rows_x, rows_y, depth),
        (8, rows_x, rows_y + 1, depth),
        (8, rows_x, rows_y, depth),
        (8, 2, 16, 256),
        (8, 2, 2, 16, 128),
        (16, 2, 16, 128),
        (16, 2, 16, 128),
        (8, 2, 2, 16, 128),
        (8, 4, 16, 128),
        (18, rows_x + 1, 16, depth),
        woven.shape,
    ]
    out = pl.pallas_call(
        functools.partial(fused_kernel, sizes),
        out_shape=jax.ShapeDtypeStruct(woven.shape, jnp.float32),
        in_specs=[pl.BlockSpec(memory_space=pltpu.HBM)] * 8,
        out_specs=pl.BlockSpec(memory_space=pltpu.HBM),
        scratch_shapes=[pltpu.VMEM(shape, jnp.float32) for shape in shapes]
        + [
            pltpu.SemaphoreType.DMA((35,)),
            pltpu.SemaphoreType.DMA((35,)),
            pltpu.SemaphoreType.DMA((8,)),
            pltpu.SemaphoreType.DMA((rows_x,)),
        ],
        compiler_params=pltpu.CompilerParams(
            collective_id=5, has_side_effects=True, vmem_limit_bytes=(64 << 20) - (1 << 19)
        ),
    )(woven, *given)
    return jnp.transpose(out.reshape(3, 3, 3, rows_x, rows_y, 2, depth), (0, 5, 1, 2, 3, 4, 6))


def shards(sizes, gauge_links):
    if sizes == (4, 2, 2):
        return fused(sizes, gauge_links)
    rows_x, rows_y, depth = gauge_links.shape[4:]
    wide, wide_back = tables()[:2]
    links = gauge_links.reshape(54, rows_x, rows_y, depth)
    first = links[:, :, 0, :]
    edge = jnp.moveaxis(jnp.concatenate([first[:18], first[36:]], axis=0), 0, 1)
    hx, hy = exchange(sizes, -1, (18, 36, 0), 1, links, edge)
    gu, lx, ly, rim = local(
        staple_kernel,
        (
            (24, rows_x, rows_y, depth),
            (16, rows_x + 1, rows_y, depth),
            (16, rows_x, rows_y + 1, depth),
            (rows_x, 16, depth),
        ),
        [(54, rows_x + 1, 16, depth)],
        links,
        hx,
        hy,
    )
    rx, ry = exchange(sizes, 1, (0, 16, rows_x), 2, lx, rim)
    smeared, blocks = local(
        functools.partial(smear_kernel, False),
        ((54, rows_x, rows_y, depth), (8, 2, 16, 256)),
        [
            (8, rows_x, rows_y, depth),
            (8, rows_x, rows_y + 1, depth),
            (8, rows_x, rows_y, depth),
            (8, 2, 16, 256),
        ],
        links,
        gu,
        lx,
        ly,
        rx,
        ry,
        wide,
    )
    used = blocks[:, :, : rows_y + 1]
    payload = jnp.concatenate([used[..., :depth], used[..., depth:]], axis=1)
    accel = general_solve(payload, rows_x, rows_y, depth)
    accel = jnp.pad(accel, ((0, 0), (0, 0), (0, 16 - accel.shape[2]), (0, 0)))
    rotated = local(
        functools.partial(rotate_kernel, False),
        (54, rows_x, rows_y, depth),
        [(8, 4, 16, 128), (18, rows_x + 1, 16, depth)],
        accel,
        smeared,
        wide_back,
    )
    return rotated.reshape(gauge_links.shape)


def solution(mesh):
    sizes = (mesh.shape["gx"], mesh.shape["gy"], mesh.shape["gz"])
    return jax.shard_map(
        functools.partial(shards, sizes),
        mesh=mesh,
        in_specs=(P(None, None, None, None, ("slices", "gx"), ("gy", "gz"), None),),
        out_specs=P(None, None, None, None, ("slices", "gx"), ("gy", "gz"), None),
        check_vma=False,
    )
```
